32 devices in a mesh: dp: 4 (over y, core), tensor: 8 (over z, x).
Axes of the slice: x: 2, y: 2, z: 4, core: 2. Of those that a mesh axis runs over, the one named last changes fastest.
Arguments:
- tokens: bfloat16 [512, 8192], P('dp', 'tensor'), may hold values from -6 to 6
- grad_out: bfloat16 [512, 8192], P('dp', 'tensor'), may hold values from -6 to 6
- packed_weight_blocks: float32 [2048, 128, 128], P(('dp', 'tensor')), may hold values from -4 to 4
- packed_first_moments: float32 [2048, 128, 128], P(('dp', 'tensor')), may hold values from -2 to 2
- packed_second_moments: float32 [2048, 128, 128], P(('dp', 'tensor')), may hold values from 0.05 to 1
- block_mask: int32 [2, 64, 128], P(None, None, 'tensor'), may hold values from 0 to 1, as said below
- last_step: int32 [2, 64, 128], P(None, None, 'tensor'), may hold values from 130 to 139
- regrown: int32 [2, 64, 128], P(None, None, 'tensor'), may hold values 0 or 1
- step_now: int32 [1], replicated, may hold values from 140 to 149
Outputs:
- input_grad: bfloat16 [512, 8192], P('dp', 'tensor')
- new_weights: float32 [2048, 128, 128], P(('dp', 'tensor'))
- new_first: float32 [2048, 128, 128], P(('dp', 'tensor'))
- new_second: float32 [2048, 128, 128], P(('dp', 'tensor'))
The draws below stay inside these ranges and needn't reach their ends.
Inputs may be any that keep to these rules, and one draw needn't show every extreme that they name: `block_mask`: within one tensor shard's 16 block columns, both matrices together hold between 128 and 256 active blocks; some shard holds exactly 256.
All inputs are finite; a program needn't handle non-finite values. No bound on the sum of `regrown` on one device may be relied on, other than what follows from the above.
Results may differ from the reference program's by a relative error of at most 0.014.
Values may be sent and summed in bfloat16 or wider, within the bound.
A program may use at most 192 MiB of HBM per device.

```python
import math
import jax
import jax.numpy as jnp
from jax import lax

D = 8192
BLOCK_SIDE = 128
TOK_DEV = 128
TOKENS = 512
DB = 64
HB = 128
HBT = 16
SLOTS = 256
DEVICE_SLOTS = 64
PACKED_SLOTS = 2048
N_DP = 4
N_TENSOR = 8


def draw_block_mask(key, part):
    count_key = jax.random.fold_in(key, 11)
    fullest_key = jax.random.fold_in(key, 12)
    order_key = jax.random.fold_in(key, 13)
    shard_blocks = 2 * DB * HBT
    counts = jax.random.randint(count_key, (N_TENSOR,), SLOTS // 2, SLOTS + 1, dtype=jnp.int32)
    fullest = jax.random.randint(fullest_key, (), 0, N_TENSOR, dtype=jnp.int32)
    counts = jnp.where(jnp.arange(N_TENSOR, dtype=jnp.int32) == fullest, SLOTS, counts)
    scores = jax.random.randint(order_key, (N_TENSOR, shard_blocks), 0, 1 << 18, dtype=jnp.int32)
    scores = scores * shard_blocks + jnp.arange(shard_blocks, dtype=jnp.int32)[None, :]
    block_ranks = jnp.argsort(jnp.argsort(scores, axis=1), axis=1)
    active = (block_ranks < counts[:, None]).astype(jnp.int32)
    layout = active.reshape(N_TENSOR, 2, DB, HBT)
    return layout.transpose(1, 2, 0, 3).reshape(2, DB, HB)


def set_ends(entries, rng, least, high):
    shape = entries.shape
    index_at = [jax.random.randint(jax.random.fold_in(rng, axis), (), 0, shape[axis]) for axis in range(len(shape))]
    entries = entries.at[tuple(index_at)].set(least)
    longest = shape.index(max(shape))
    index_at[longest] = (index_at[longest] + 1) % shape[longest]
    return entries.at[tuple(index_at)].set(high)


def level_of(rng, shape, shards, low, high):
    level = 1.0
    for dim, blocks in shards:
        steps = jax.random.uniform(jax.random.fold_in(jax.random.fold_in(rng, 6), dim), (blocks,), jnp.float32, low / len(shards), high / len(shards))
        level = level * jnp.repeat(jnp.exp(steps), shape[dim] // blocks).reshape((-1,) + (1,) * (len(shape) - 1 - dim))
    return level


def centred(rng, dims, deviation, bound, shards=(), kind=jnp.bfloat16):
    entries = deviation * jax.random.normal(rng, dims, jnp.float32)
    if shards:
        entries = entries * level_of(rng, dims, shards, -0.22, 0.18)
    return jnp.clip(entries, -bound, bound).astype(kind)


def setup_inputs(seed: int = 0) -> dict:
    arg_keys = jax.random.split(jax.random.key(seed), 10)
    return {
        "tokens": centred(arg_keys[0], (TOKENS, D), 1.0, 6.0, ((0, 4), (1, 8))),
        "grad_out": centred(arg_keys[1], (TOKENS, D), 1.0, 6.0, ((0, 4), (1, 8))),
        "packed_weight_blocks": centred(arg_keys[2], (PACKED_SLOTS, BLOCK_SIDE, BLOCK_SIDE), 1.0, 4.0, ((0, 32),), jnp.float32),
        "packed_first_moments": centred(arg_keys[3], (PACKED_SLOTS, BLOCK_SIDE, BLOCK_SIDE), 0.3, 2.0, ((0, 32),), jnp.float32),
        "packed_second_moments": jnp.clip(jnp.exp(math.log(1.0) - 2.9957323 * jax.random.uniform(arg_keys[4], (PACKED_SLOTS, BLOCK_SIDE, BLOCK_SIDE), jnp.float32) ** level_of(arg_keys[4], (PACKED_SLOTS, BLOCK_SIDE, BLOCK_SIDE), ((0, 32),), -0.2, 0.2)), 0.05, 1.0),
        "block_mask": draw_block_mask(jax.random.fold_in(arg_keys[9], 71), 0),
        "last_step": set_ends(jax.random.randint(arg_keys[6], (2, DB, HB), 130, 140), jax.random.fold_in(arg_keys[6], 1), 130, 139).astype(jnp.int32),
        "regrown": set_ends((jax.random.randint(arg_keys[7], (2, DB, HB), 0, 5) < 1).astype(jnp.int32), jax.random.fold_in(arg_keys[7], 1), 0, 1),
        "step_now": jax.random.randint(arg_keys[8], (1,), 140, 150).astype(jnp.int32),
    }


beta_one = 0.9
beta_two = 0.95
learn_rate = 0.05
decay_rate = 0.1
epsilon = 0.05

def silu_slope(values):
    sigmoid = jax.nn.sigmoid(values)
    return sigmoid * (1.0 + values * (1.0 - sigmoid))

def slot_table(mask_grid, regrown_grid, last_grid, slot_total):
    flags = mask_grid.reshape(-1)
    numbered = jnp.cumsum(flags, dtype=jnp.int32) - 1
    block_total = flags.shape[0]
    matches = (numbered[None, :] == jnp.arange(slot_total, dtype=jnp.int32)[:, None]) & (flags[None, :] == 1)
    block_index = lax.optimization_barrier(jnp.sum(jnp.where(matches, jnp.arange(block_total, dtype=jnp.int32)[None, :], 0), axis=1, dtype=jnp.int32))
    slot_regrown = lax.optimization_barrier(jnp.sum(jnp.where(matches, regrown_grid.reshape(-1)[None, :], 0), axis=1, dtype=jnp.int32))
    slot_last = lax.optimization_barrier(jnp.sum(jnp.where(matches, last_grid.reshape(-1)[None, :], 0), axis=1, dtype=jnp.int32))
    live_count = jnp.sum(flags, dtype=jnp.int32)
    return (numbered, block_index, slot_regrown, slot_last, live_count)

def adam_step(weights, first_in, second_in, block_grads, live_slots, slot_regrown, slot_last, step_value):
    regrown_now = (slot_regrown == 1)[:, None, None]
    skipped = (step_value - slot_last - 1).astype(jnp.float32)[:, None, None]
    base_weight = jnp.where(regrown_now, jnp.float32(0.0), weights)
    kept_first = jnp.where(regrown_now, jnp.float32(0.0), first_in * jnp.power(jnp.float32(beta_one), skipped))
    kept_second = jnp.where(regrown_now, jnp.float32(0.0), second_in * jnp.power(jnp.float32(beta_two), skipped))
    new_first = beta_one * kept_first + (1.0 - beta_one) * block_grads
    new_second = beta_two * kept_second + (1.0 - beta_two) * block_grads * block_grads
    bias_count = jnp.where(regrown_now, jnp.float32(1.0), step_value.astype(jnp.float32) + jnp.zeros_like(skipped))
    first_hat = new_first / (1.0 - jnp.power(jnp.float32(beta_one), bias_count))
    second_hat = new_second / (1.0 - jnp.power(jnp.float32(beta_two), bias_count))
    new_weight = base_weight - learn_rate * (first_hat / (jnp.sqrt(second_hat) + epsilon) + decay_rate * base_weight)
    keep_slot = live_slots[:, None, None]
    return (jnp.where(keep_slot, new_weight, weights), jnp.where(keep_slot, new_first, first_in), jnp.where(keep_slot, new_second, second_in))

def reference(tokens, grad_out, packed_weight_blocks, packed_first_moments, packed_second_moments, block_mask, last_step, regrown, step_now):
    scale_factor = 3.0 / math.sqrt(D)
    step_value = step_now[0]

    def by_shard(packed_array):
        return packed_array.reshape(N_DP, N_TENSOR, DEVICE_SLOTS, BLOCK_SIDE, BLOCK_SIDE).transpose(1, 0, 2, 3, 4).reshape(N_TENSOR, SLOTS, BLOCK_SIDE, BLOCK_SIDE)

    def grid_shard(layout):
        return layout.reshape(2, DB, N_TENSOR, HBT).transpose(2, 0, 1, 3)

    def unshard(stacked_blocks):
        return stacked_blocks.reshape(N_TENSOR, N_DP, DEVICE_SLOTS, BLOCK_SIDE, BLOCK_SIDE).transpose(1, 0, 2, 3, 4).reshape(PACKED_SLOTS, BLOCK_SIDE, BLOCK_SIDE)

    def shard_step(accum, shard_in):
        weights_s, first_s, second_s, mask_s, last_s, regrown_s = shard_in
        numbered, block_index, slot_regrown, slot_last, live_count = slot_table(mask_s, regrown_s, last_s, SLOTS)
        usable = (mask_s.reshape(-1) == 1) & (regrown_s.reshape(-1) == 0)
        packed = weights_s.astype(jnp.bfloat16)
        dense = jnp.take(packed, jnp.maximum(numbered, 0), axis=0)
        dense = jnp.where(usable[:, None, None], dense, jnp.zeros((), jnp.bfloat16))
        dense = dense.reshape(2, DB, HBT, BLOCK_SIDE, BLOCK_SIDE).transpose(0, 1, 3, 2, 4).reshape(2, D, HBT * BLOCK_SIDE)
        pre_act = scale_factor * jnp.dot(tokens, dense[0], preferred_element_type=jnp.float32)
        back_act = scale_factor * jnp.dot(grad_out, dense[1], preferred_element_type=jnp.float32)
        hidden = jax.nn.silu(pre_act).astype(jnp.bfloat16)
        hidden_grad = (back_act * silu_slope(pre_act)).astype(jnp.bfloat16)
        partial_value = (scale_factor * jnp.dot(hidden_grad, dense[0].T, preferred_element_type=jnp.float32)).astype(jnp.bfloat16)
        accum = accum + partial_value.astype(jnp.float32)
        left_source = jnp.concatenate([tokens.reshape(TOKENS, DB, BLOCK_SIDE), grad_out.reshape(TOKENS, DB, BLOCK_SIDE)], axis=1)
        right_source = jnp.concatenate([hidden_grad.reshape(TOKENS, HBT, BLOCK_SIDE), hidden.reshape(TOKENS, HBT, BLOCK_SIDE)], axis=1)
        matrix_of = block_index // (DB * HBT)
        row_of = block_index // HBT % DB
        column_of = block_index % HBT
        left_rows = jnp.take(left_source, (matrix_of * DB + row_of).astype(jnp.int32), axis=1)
        right_rows = jnp.take(right_source, (matrix_of * HBT + column_of).astype(jnp.int32), axis=1)
        left_groups = left_rows.astype(jnp.float32).reshape(N_DP, TOK_DEV, SLOTS, BLOCK_SIDE)
        right_groups = right_rows.astype(jnp.float32).reshape(N_DP, TOK_DEV, SLOTS, BLOCK_SIDE)
        group_tiles = (scale_factor * jnp.einsum('gtsi,gtsj->gsij', left_groups, right_groups)).astype(jnp.bfloat16)
        block_grads = lax.optimization_barrier(jnp.sum(group_tiles.astype(jnp.float32), axis=0))
        live_slots = jnp.arange(SLOTS, dtype=jnp.int32) < live_count
        updated = adam_step(weights_s, first_s, second_s, block_grads, live_slots, slot_regrown, slot_last, step_value)
        return (accum, updated)
    shard_inputs = (by_shard(packed_weight_blocks), by_shard(packed_first_moments), by_shard(packed_second_moments), grid_shard(block_mask), grid_shard(last_step), grid_shard(regrown))
    accum, updated = lax.scan(shard_step, jnp.zeros((TOKENS, D), jnp.float32), shard_inputs)
    new_weights, new_first, new_second = updated
    return (accum.astype(jnp.bfloat16), unshard(new_weights), unshard(new_first), unshard(new_second))
```

```python
import functools
import math

import jax
import jax.numpy as jnp
from jax import lax
from jax.experimental import pallas as pl
from jax.experimental.pallas import tpu as pltpu
from jax.sharding import PartitionSpec as P

D = 8192


beta_one = 0.9
beta_two = 0.95
learn_rate = 0.05
decay_rate = 0.1
epsilon = 0.05


def silu_slope(values):
    sigmoid = jax.nn.sigmoid(values)
    return sigmoid * (1.0 + values * (1.0 - sigmoid))


def slot_table(mask_grid, regrown_grid, last_grid, slot_total):
    flags = mask_grid.reshape(-1)
    numbered = jnp.cumsum(flags, dtype=jnp.int32) - 1
    block_total = flags.shape[0]
    matches = (numbered[None, :] == jnp.arange(slot_total, dtype=jnp.int32)[:, None]) & (
        flags[None, :] == 1
    )
    block_index = jnp.sum(
        jnp.where(matches, jnp.arange(block_total, dtype=jnp.int32)[None, :], 0),
        axis=1,
        dtype=jnp.int32,
    )
    slot_regrown = jnp.sum(
        jnp.where(matches, regrown_grid.reshape(-1)[None, :], 0), axis=1, dtype=jnp.int32
    )
    slot_last = jnp.sum(
        jnp.where(matches, last_grid.reshape(-1)[None, :], 0), axis=1, dtype=jnp.int32
    )
    live_count = jnp.sum(flags, dtype=jnp.int32)
    return (numbered, block_index, slot_regrown, slot_last, live_count)


def adam_step(
    weights, first_in, second_in, block_grads, live_slots, slot_regrown, slot_last, step_value
):
    regrown_now = (slot_regrown == 1)[:, None, None]
    skipped = (step_value - slot_last - 1).astype(jnp.float32)[:, None, None]
    base_weight = jnp.where(regrown_now, jnp.float32(0.0), weights)
    kept_first = jnp.where(
        regrown_now, jnp.float32(0.0), first_in * jnp.power(jnp.float32(beta_one), skipped)
    )
    kept_second = jnp.where(
        regrown_now, jnp.float32(0.0), second_in * jnp.power(jnp.float32(beta_two), skipped)
    )
    new_first = beta_one * kept_first + (1.0 - beta_one) * block_grads
    new_second = beta_two * kept_second + (1.0 - beta_two) * block_grads * block_grads
    bias_count = jnp.where(
        regrown_now, jnp.float32(1.0), step_value.astype(jnp.float32) + jnp.zeros_like(skipped)
    )
    first_hat = new_first / (1.0 - jnp.power(jnp.float32(beta_one), bias_count))
    second_hat = new_second / (1.0 - jnp.power(jnp.float32(beta_two), bias_count))
    new_weight = base_weight - learn_rate * (
        first_hat / (jnp.sqrt(second_hat) + epsilon) + decay_rate * base_weight
    )
    keep_slot = live_slots[:, None, None]
    return (
        jnp.where(keep_slot, new_weight, weights),
        jnp.where(keep_slot, new_first, first_in),
        jnp.where(keep_slot, new_second, second_in),
    )


def gather_all(own_packed, own_left):
    packed = lax.all_gather(own_packed, "dp", axis=0, tiled=True)
    left_source = lax.all_gather(own_left, "tensor", axis=0, tiled=True)
    return packed, left_source


def reduce_all(tiles, partial_rows):
    block_grads = lax.psum_scatter(tiles, "dp", scatter_dimension=0, tiled=True)
    summed_rows = lax.psum_scatter(partial_rows, "tensor", scatter_dimension=0, tiled=True)
    return block_grads.astype(jnp.float32), summed_rows.astype(jnp.float32)


UNROLL = 4


def forward_kernel(
    left_at, right_at, sum_at, packed_ref, left_ref, right_ref, tiles_ref, sums, *, scale
):
    slot_total = packed_ref.shape[0]
    columns = right_ref.shape[0] // 2

    def clear(index, carry):
        sums[index] = jnp.zeros(sums.shape[1:], jnp.float32)
        return carry

    lax.fori_loop(0, sums.shape[0], clear, 0)

    def add_slots(step, carry):
        base = step * UNROLL
        parts = [
            jnp.dot(
                left_ref[left_at[base + k]],
                packed_ref[base + k],
                preferred_element_type=jnp.float32,
            )
            for k in range(UNROLL)
        ]
        for k in range(UNROLL):
            sums[sum_at[base + k]] += parts[k]
        return carry

    lax.fori_loop(0, slot_total // UNROLL, add_slots, 0)

    def activate(column, carry):
        pre_act = scale * sums[column]
        back_act = scale * sums[columns + column]
        right_ref[column] = (back_act * silu_slope(pre_act)).astype(jnp.bfloat16)
        right_ref[columns + column] = jax.nn.silu(pre_act).astype(jnp.bfloat16)
        return carry

    lax.fori_loop(0, columns, activate, 0)

    def make_tiles(step, carry):
        base = step * UNROLL
        for k in range(UNROLL):
            tile = lax.dot_general(
                left_ref[left_at[base + k]],
                right_ref[right_at[base + k]],
                (((0,), (0,)), ((), ())),
                preferred_element_type=jnp.float32,
            )
            tiles_ref[base + k] = (scale * tile).astype(jnp.bfloat16)
        return carry

    lax.fori_loop(0, slot_total // UNROLL, make_tiles, 0)


def input_grad_kernel(right_at, row_at, up_steps, packed_ref, right_ref, out_ref, sums, *, scale):
    rows = out_ref.shape[0]

    def clear(index, carry):
        sums[index] = jnp.zeros(sums.shape[1:], jnp.float32)
        return carry

    lax.fori_loop(0, rows, clear, 0)

    def add_slots(step, carry):
        base = step * UNROLL
        parts = [
            lax.dot_general(
                right_ref[right_at[base + k]],
                packed_ref[base + k],
                (((1,), (1,)), ((), ())),
                preferred_element_type=jnp.float32,
            )
            for k in range(UNROLL)
        ]
        for k in range(UNROLL):
            sums[row_at[base + k]] += parts[k]
        return carry

    lax.fori_loop(0, up_steps[0], add_slots, 0)

    def finish(index, carry):
        out_ref[index] = (scale * sums[index]).astype(jnp.bfloat16)
        return carry

    lax.fori_loop(0, rows, finish, 0)


def per_device(
    tokens,
    grad_out,
    packed_weight_blocks,
    packed_first_moments,
    packed_second_moments,
    block_mask,
    last_step,
    regrown,
    step_now,
):
    scale_factor = 3.0 / math.sqrt(D)
    tok_count = tokens.shape[0]
    owned_slots = packed_weight_blocks.shape[0]
    block_size = packed_weight_blocks.shape[1]
    row_blocks = block_mask.shape[1]
    column_blocks = block_mask.shape[2]
    local_rows = tokens.shape[1] // block_size
    groups = lax.axis_size("dp")
    slot_total = owned_slots * groups
    step_value = step_now[0]
    own_left = jnp.concatenate(
        [
            tokens.reshape(tok_count, local_rows, block_size),
            grad_out.reshape(tok_count, local_rows, block_size),
        ],
        axis=1,
    ).transpose(1, 0, 2)
    own_packed = packed_weight_blocks.astype(jnp.bfloat16)
    packed, left_source = gather_all(own_packed, own_left)
    _, block_index, slot_regrown, slot_last, live_count = slot_table(
        block_mask, regrown, last_step, slot_total
    )
    matrix_of = block_index // (row_blocks * column_blocks)
    row_of = block_index // column_blocks % row_blocks
    column_of = block_index % column_blocks
    slot_ids = jnp.arange(slot_total, dtype=jnp.int32)
    usable = (slot_ids < live_count) & (slot_regrown == 0)
    left_at = (row_of // local_rows * 2 + matrix_of) * local_rows + row_of % local_rows
    right_at = matrix_of * column_blocks + column_of
    sum_at = jnp.where(usable, right_at, 2 * column_blocks)
    row_at = jnp.where(usable & (matrix_of == 0), row_of, row_blocks)
    up_count = jnp.sum(block_mask[0], dtype=jnp.int32)
    up_steps = ((up_count + UNROLL - 1) // UNROLL).reshape(1)
    smem = pl.BlockSpec(memory_space=pltpu.SMEM)
    vmem = pl.BlockSpec(memory_space=pltpu.VMEM)
    params = pltpu.CompilerParams(vmem_limit_bytes=48 * 1024 * 1024)
    block = (tok_count, block_size)
    right_source, tiles = pl.pallas_call(
        functools.partial(forward_kernel, scale=scale_factor),
        out_shape=(
            jax.ShapeDtypeStruct((2 * column_blocks,) + block, jnp.bfloat16),
            jax.ShapeDtypeStruct((slot_total, block_size, block_size), jnp.bfloat16),
        ),
        in_specs=[smem] * 3 + [vmem] * 2,
        out_specs=(vmem, vmem),
        scratch_shapes=[pltpu.VMEM((2 * column_blocks + 1,) + block, jnp.float32)],
        compiler_params=params,
    )(left_at, right_at, sum_at, packed, left_source)
    partial_rows = pl.pallas_call(
        functools.partial(input_grad_kernel, scale=scale_factor),
        out_shape=jax.ShapeDtypeStruct((row_blocks,) + block, jnp.bfloat16),
        in_specs=[smem] * 3 + [vmem] * 2,
        out_specs=vmem,
        scratch_shapes=[pltpu.VMEM((row_blocks + 1,) + block, jnp.float32)],
        compiler_params=params,
    )(right_at, row_at, up_steps, packed, right_source)
    block_grads, summed_rows = reduce_all(tiles, partial_rows)
    input_grad = (
        summed_rows.transpose(1, 0, 2).reshape(tok_count, tokens.shape[1]).astype(jnp.bfloat16)
    )
    owner_first = lax.axis_index("dp") * owned_slots
    mine_regrown = lax.dynamic_slice_in_dim(slot_regrown, owner_first, owned_slots)
    mine_last = lax.dynamic_slice_in_dim(slot_last, owner_first, owned_slots)
    live_slots = owner_first + jnp.arange(owned_slots, dtype=jnp.int32) < live_count
    new_weights, new_first, new_second = adam_step(
        packed_weight_blocks,
        packed_first_moments,
        packed_second_moments,
        block_grads,
        live_slots,
        mine_regrown,
        mine_last,
        step_value,
    )
    return (input_grad, new_weights, new_first, new_second)


def solution(mesh):
    in_specs = (
        P("dp", "tensor"),
        P("dp", "tensor"),
        P(("dp", "tensor"), None, None),
        P(("dp", "tensor"), None, None),
        P(("dp", "tensor"), None, None),
        P(None, None, "tensor"),
        P(None, None, "tensor"),
        P(None, None, "tensor"),
        P(),
    )
    out_specs = (
        P("dp", "tensor"),
        P(("dp", "tensor"), None, None),
        P(("dp", "tensor"), None, None),
        P(("dp", "tensor"), None, None),
    )
    return jax.shard_map(
        per_device, mesh=mesh, in_specs=in_specs, out_specs=out_specs, check_vma=False
    )
```

```python
import functools
import math

import jax
import jax.numpy as jnp
from jax import lax
from jax.experimental import pallas as pl
from jax.experimental.pallas import tpu as pltpu
from jax.sharding import PartitionSpec as P

D = 8192


beta_one = 0.9
beta_two = 0.95
learn_rate = 0.05
decay_rate = 0.1
epsilon = 0.05


def silu_slope(values):
    sigmoid = jax.nn.sigmoid(values)
    return sigmoid * (1.0 + values * (1.0 - sigmoid))


def slot_table(mask_grid, regrown_grid, last_grid, slot_total):
    flags = mask_grid.reshape(-1)
    numbered = jnp.cumsum(flags, dtype=jnp.int32) - 1
    block_total = flags.shape[0]
    matches = (numbered[None, :] == jnp.arange(slot_total, dtype=jnp.int32)[:, None]) & (
        flags[None, :] == 1
    )
    block_index = jnp.sum(
        jnp.where(matches, jnp.arange(block_total, dtype=jnp.int32)[None, :], 0),
        axis=1,
        dtype=jnp.int32,
    )
    slot_regrown = jnp.sum(
        jnp.where(matches, regrown_grid.reshape(-1)[None, :], 0), axis=1, dtype=jnp.int32
    )
    slot_last = jnp.sum(
        jnp.where(matches, last_grid.reshape(-1)[None, :], 0), axis=1, dtype=jnp.int32
    )
    live_count = jnp.sum(flags, dtype=jnp.int32)
    return (numbered, block_index, slot_regrown, slot_last, live_count)


def adam_step(
    weights, first_in, second_in, block_grads, live_slots, slot_regrown, slot_last, step_value
):
    regrown_now = (slot_regrown == 1)[:, None, None]
    skipped = (step_value - slot_last - 1).astype(jnp.float32)[:, None, None]
    base_weight = jnp.where(regrown_now, jnp.float32(0.0), weights)
    kept_first = jnp.where(
        regrown_now, jnp.float32(0.0), first_in * jnp.power(jnp.float32(beta_one), skipped)
    )
    kept_second = jnp.where(
        regrown_now, jnp.float32(0.0), second_in * jnp.power(jnp.float32(beta_two), skipped)
    )
    new_first = beta_one * kept_first + (1.0 - beta_one) * block_grads
    new_second = beta_two * kept_second + (1.0 - beta_two) * block_grads * block_grads
    bias_count = jnp.where(
        regrown_now, jnp.float32(1.0), step_value.astype(jnp.float32) + jnp.zeros_like(skipped)
    )
    first_hat = new_first / (1.0 - jnp.power(jnp.float32(beta_one), bias_count))
    second_hat = new_second / (1.0 - jnp.power(jnp.float32(beta_two), bias_count))
    new_weight = base_weight - learn_rate * (
        first_hat / (jnp.sqrt(second_hat) + epsilon) + decay_rate * base_weight
    )
    keep_slot = live_slots[:, None, None]
    return (
        jnp.where(keep_slot, new_weight, weights),
        jnp.where(keep_slot, new_first, first_in),
        jnp.where(keep_slot, new_second, second_in),
    )


INNER = 2


def piece(index, chunk, chunks, shard):
    size = shard // chunks
    return pl.ds((index * chunks + chunk) * size, size)


def remote(src, dst, send_sem, recv_sem, axis, target):
    return pltpu.make_async_remote_copy(
        src_ref=src,
        dst_ref=dst,
        send_sem=send_sem,
        recv_sem=recv_sem,
        device_id={axis: target},
        device_id_type=pl.DeviceIdType.MESH,
    )


def greet(targets):
    barrier = pltpu.get_barrier_semaphore()
    for axis, target, exists in targets:

        @pl.when(exists)
        def _(axis=axis, target=target):
            pl.semaphore_signal(
                barrier, inc=1, device_id={axis: target}, device_id_type=pl.DeviceIdType.MESH
            )

    pl.semaphore_wait(barrier, sum(jnp.where(exists, 1, 0) for _, _, exists in targets))


class LineGather:
    def __init__(self, axis, size, chunks, own, out, sems):
        self.axis, self.chunks, self.own, self.out = axis, chunks, own, out
        self.recv, self.up, self.down, self.across, self.local = sems
        self.outer = size // INNER
        me = lax.axis_index(axis)
        self.me, self.mine, self.inner = me, me // INNER, me % INNER
        self.shard = own.shape[0]

    def targets(self):
        mine = self.mine
        return [
            (self.axis, self.me + INNER, mine + 1 < self.outer),
            (self.axis, self.me - INNER, mine > 0),
            (self.axis, mine * INNER + 1 - self.inner, mine >= 0),
        ]

    def copy(self, source, chunk, way, inner=None):
        inner = self.inner if inner is None else inner
        index = source * INNER + inner
        at = self.out.at[piece(index, chunk, self.chunks, self.shard)]
        slot = source * self.chunks + chunk
        sem, target = {
            "up": (self.up, self.me + INNER),
            "down": (self.down, self.me - INNER),
            "across": (self.across, self.mine * INNER + 1 - self.inner),
        }[way]
        recv = self.recv.at[index * self.chunks + chunk]
        return at, sem.at[slot], recv, target

    def send(self, source, chunk, way, own=False):
        at, sem, recv, target = self.copy(source, chunk, way)
        src = self.own.at[piece(0, chunk, self.chunks, self.shard)] if own else at
        remote(src, at, sem, recv, self.axis, target).start()

    def wait_send(self, source, chunk, way):
        at, sem, recv, target = self.copy(source, chunk, way)
        remote(at, at, sem, recv, self.axis, target).wait_send()

    def wait_recv(self, source, chunk, inner):
        at, sem, recv, target = self.copy(source, chunk, "across", inner)
        remote(at, at, sem, recv, self.axis, target).wait_recv()

    def own_copy(self):
        at = self.out.at[pl.ds(self.me * self.shard, self.shard)]
        return pltpu.make_async_copy(self.own, at, self.local)

    def begin(self, chunk):
        mine = self.mine

        @pl.when(mine + 1 < self.outer)
        def _():
            self.send(mine, chunk, "up", own=True)

        @pl.when(mine > 0)
        def _():
            self.send(mine, chunk, "down", own=True)

        self.send(mine, chunk, "across", own=True)

    def step(self, distance, chunk):
        low, high = self.mine - distance, self.mine + distance

        @pl.when(low >= 0)
        def _():
            self.wait_recv(low, chunk, self.inner)

            @pl.when(self.mine + 1 < self.outer)
            def _():
                self.send(low, chunk, "up")

            self.send(low, chunk, "across")

        @pl.when(high < self.outer)
        def _():
            self.wait_recv(high, chunk, self.inner)

            @pl.when(self.mine > 0)
            def _():
                self.send(high, chunk, "down")

            self.send(high, chunk, "across")

    def finish(self):
        for source in range(self.outer):
            for chunk in range(self.chunks):
                self.wait_recv(source, chunk, 1 - self.inner)
                self.wait_send(source, chunk, "across")

                @pl.when((self.mine >= source) & (self.mine + 1 < self.outer))
                def _(source=source, chunk=chunk):
                    self.wait_send(source, chunk, "up")

                @pl.when((self.mine <= source) & (self.mine > 0))
                def _(source=source, chunk=chunk):
                    self.wait_send(source, chunk, "down")

        self.own_copy().wait()


def gather_kernel(sizes, chunk_counts, own_packed, own_left, packed_out, left_out, *sems):
    lines = [
        LineGather("dp", sizes[0], chunk_counts[0], own_packed, packed_out, sems[:5]),
        LineGather("tensor", sizes[1], chunk_counts[1], own_left, left_out, sems[5:]),
    ]
    greet(lines[0].targets() + lines[1].targets())
    events = []
    for line in lines:
        for chunk in range(line.chunks):
            events.append((chunk / line.chunks, line, 0, chunk))
            for distance in range(1, line.outer):
                when = 1 + (distance - 1 + (chunk + 1) / line.chunks) / (line.outer - 1)
                events.append((when, line, distance, chunk))
    events.sort(key=lambda event: event[0])
    for when, line, distance, chunk in events:
        if distance == 0:
            line.begin(chunk)
    for line in lines:
        line.own_copy().start()
    for when, line, distance, chunk in events:
        if distance > 0:
            line.step(distance, chunk)
    for line in lines:
        line.finish()


def line_sems(size, chunks):
    dma = pltpu.SemaphoreType.DMA
    outer = size // INNER
    return [dma((size * chunks,))] + [dma((outer * chunks,))] * 3 + [dma]


def gather_all(own_packed, own_left):
    sizes = (lax.axis_size("dp"), lax.axis_size("tensor"))
    chunk_counts = (math.gcd(4, own_packed.shape[0]), math.gcd(2, own_left.shape[0]))
    vmem = pl.BlockSpec(memory_space=pltpu.VMEM)
    return pl.pallas_call(
        functools.partial(gather_kernel, sizes, chunk_counts),
        out_shape=(
            jax.ShapeDtypeStruct((sizes[0] * own_packed.shape[0],) + own_packed.shape[1:], jnp.bfloat16),
            jax.ShapeDtypeStruct((sizes[1] * own_left.shape[0],) + own_left.shape[1:], jnp.bfloat16),
        ),
        in_specs=[vmem, vmem],
        out_specs=(pl.BlockSpec(memory_space=pl.ANY), pl.BlockSpec(memory_space=pl.ANY)),
        scratch_shapes=line_sems(sizes[0], chunk_counts[0]) + line_sems(sizes[1], chunk_counts[1]),
        compiler_params=pltpu.CompilerParams(
            collective_id=0, has_side_effects=True, vmem_limit_bytes=48 * 1024 * 1024
        ),
    )(own_packed, own_left)


class PairReduce:
    def __init__(self, axis, size, chunks, data, out, near, far, sems):
        self.axis, self.chunks, self.data, self.out = axis, chunks, data, out
        self.near, self.far = near, far
        self.near_send, self.near_recv, self.far_send, self.far_recv = sems
        self.outer = size // INNER
        me = lax.axis_index(axis)
        self.me, self.mine, self.inner = me, me // INNER, me % INNER
        self.shard = out.shape[0]

    def owner(self, offset):
        return lax.rem(self.mine + offset, self.outer)

    def targets(self):
        far = [
            (self.axis, self.owner(offset) * INNER + self.inner, self.mine >= 0)
            for offset in range(1, self.outer)
        ]
        return far + [(self.axis, self.mine * INNER + 1 - self.inner, self.mine >= 0)]

    def near_copy(self, offset, chunk):
        owner = self.owner(offset)
        other = 1 - self.inner
        slot = owner * self.chunks + chunk
        return remote(
            self.data.at[piece(owner * INNER + other, chunk, self.chunks, self.shard)],
            self.near.at[piece(owner, chunk, self.chunks, self.shard)],
            self.near_send.at[slot],
            self.near_recv.at[slot],
            self.axis,
            self.mine * INNER + other,
        )

    def far_copy(self, offset, chunk):
        owner = self.owner(offset)
        return remote(
            self.near.at[piece(owner, chunk, self.chunks, self.shard)],
            self.far.at[piece(offset - 1, chunk, self.chunks, self.shard)],
            self.far_send.at[(offset - 1) * self.chunks + chunk],
            self.far_recv.at[(offset - 1) * self.chunks + chunk],
            self.axis,
            owner * INNER + self.inner,
        )

    def send_pair(self, offset, chunk):
        self.near_copy(offset, chunk).wait_recv()
        owner = self.owner(offset)
        size = self.shard // self.chunks
        near_at = (owner * self.chunks + chunk) * size
        data_at = ((owner * INNER + self.inner) * self.chunks + chunk) * size

        def add(index, carry):
            total = self.near[near_at + index].astype(jnp.float32)
            total += self.data[data_at + index].astype(jnp.float32)
            self.near[near_at + index] = total.astype(jnp.bfloat16)
            return carry

        lax.fori_loop(0, size, add, 0)
        self.far_copy(offset, chunk).start()

    def total(self, chunk):
        self.near_copy(0, chunk).wait_recv()
        for offset in range(1, self.outer):
            self.far_copy(offset, chunk).wait_recv()
        size = self.shard // self.chunks
        near_at = (self.mine * self.chunks + chunk) * size
        data_at = (self.me * self.chunks + chunk) * size

        def add(index, carry):
            total = self.near[near_at + index].astype(jnp.float32)
            total += self.data[data_at + index].astype(jnp.float32)
            for offset in range(1, self.outer):
                at = ((offset - 1) * self.chunks + chunk) * size
                total += self.far[at + index].astype(jnp.float32)
            self.out[chunk * size + index] = total.astype(self.out.dtype)
            return carry

        lax.fori_loop(0, size, add, 0)

    def finish(self):
        for chunk in range(self.chunks):
            for offset in range(self.outer):
                self.near_copy(offset, chunk).wait_send()
                if offset > 0:
                    self.far_copy(offset, chunk).wait_send()


def reduce_kernel(sizes, chunk_counts, tiles, rows, grads_out, rows_out, *scratch):
    wide = PairReduce(
        "dp", sizes[0], chunk_counts[0], tiles, grads_out, scratch[0], scratch[1], scratch[4:8]
    )
    thin = PairReduce(
        "tensor", sizes[1], chunk_counts[1], rows, rows_out, scratch[2], scratch[3], scratch[8:]
    )
    greet(wide.targets() + thin.targets())
    for line in (wide, thin):
        for offset in list(range(1, line.outer)) + [0]:
            for chunk in range(line.chunks):
                line.near_copy(offset, chunk).start()
    for line in (wide, thin):
        for offset in range(1, line.outer):
            for chunk in range(line.chunks):
                line.send_pair(offset, chunk)
    for chunk in range(wide.chunks - 1):
        wide.total(chunk)
    for chunk in range(thin.chunks):
        thin.total(chunk)
    wide.total(wide.chunks - 1)
    wide.finish()
    thin.finish()


def pair_sems(size, chunks):
    dma = pltpu.SemaphoreType.DMA
    outer = size // INNER
    return [dma((outer * chunks,))] * 2 + [dma((max(outer - 1, 1) * chunks,))] * 2


def reduce_all(tiles, partial_rows):
    sizes = (lax.axis_size("dp"), lax.axis_size("tensor"))
    shards = (tiles.shape[0] // sizes[0], partial_rows.shape[0] // sizes[1])
    chunk_counts = (math.gcd(4, shards[0]), math.gcd(2, shards[1]))
    vmem = pl.BlockSpec(memory_space=pltpu.VMEM)
    scratch = []
    for array, size, shard in zip((tiles, partial_rows), sizes, shards):
        outer = size // INNER
        scratch.append(pltpu.VMEM((outer * shard,) + array.shape[1:], jnp.bfloat16))
        scratch.append(pltpu.VMEM((max(outer - 1, 1) * shard,) + array.shape[1:], jnp.bfloat16))
    return pl.pallas_call(
        functools.partial(reduce_kernel, sizes, chunk_counts),
        out_shape=(
            jax.ShapeDtypeStruct((shards[0],) + tiles.shape[1:], jnp.float32),
            jax.ShapeDtypeStruct((shards[1],) + partial_rows.shape[1:], jnp.bfloat16),
        ),
        in_specs=[vmem, vmem],
        out_specs=(vmem, vmem),
        scratch_shapes=scratch
        + pair_sems(sizes[0], chunk_counts[0])
        + pair_sems(sizes[1], chunk_counts[1]),
        compiler_params=pltpu.CompilerParams(
            collective_id=1, has_side_effects=True, vmem_limit_bytes=48 * 1024 * 1024
        ),
    )(tiles, partial_rows)


UNROLL = 4


def forward_kernel(
    left_at, right_at, sum_at, packed_ref, left_ref, right_ref, tiles_ref, sums, *, scale
):
    slot_total = packed_ref.shape[0]
    columns = right_ref.shape[0] // 2

    def clear(index, carry):
        sums[index] = jnp.zeros(sums.shape[1:], jnp.float32)
        return carry

    lax.fori_loop(0, sums.shape[0], clear, 0)

    def add_slots(step, carry):
        base = step * UNROLL
        parts = [
            jnp.dot(
                left_ref[left_at[base + k]],
                packed_ref[base + k],
                preferred_element_type=jnp.float32,
            )
            for k in range(UNROLL)
        ]
        for k in range(UNROLL):
            sums[sum_at[base + k]] += parts[k]
        return carry

    lax.fori_loop(0, slot_total // UNROLL, add_slots, 0)

    def activate(column, carry):
        pre_act = scale * sums[column]
        back_act = scale * sums[columns + column]
        right_ref[column] = (back_act * silu_slope(pre_act)).astype(jnp.bfloat16)
        right_ref[columns + column] = jax.nn.silu(pre_act).astype(jnp.bfloat16)
        return carry

    lax.fori_loop(0, columns, activate, 0)

    def make_tiles(step, carry):
        base = step * UNROLL
        for k in range(UNROLL):
            tile = lax.dot_general(
                left_ref[left_at[base + k]],
                right_ref[right_at[base + k]],
                (((0,), (0,)), ((), ())),
                preferred_element_type=jnp.float32,
            )
            tiles_ref[base + k] = (scale * tile).astype(jnp.bfloat16)
        return carry

    lax.fori_loop(0, slot_total // UNROLL, make_tiles, 0)


def input_grad_kernel(right_at, row_at, up_steps, packed_ref, right_ref, out_ref, sums, *, scale):
    rows = out_ref.shape[0]

    def clear(index, carry):
        sums[index] = jnp.zeros(sums.shape[1:], jnp.float32)
        return carry

    lax.fori_loop(0, rows, clear, 0)

    def add_slots(step, carry):
        base = step * UNROLL
        parts = [
            lax.dot_general(
                right_ref[right_at[base + k]],
                packed_ref[base + k],
                (((1,), (1,)), ((), ())),
                preferred_element_type=jnp.float32,
            )
            for k in range(UNROLL)
        ]
        for k in range(UNROLL):
            sums[row_at[base + k]] += parts[k]
        return carry

    lax.fori_loop(0, up_steps[0], add_slots, 0)

    def finish(index, carry):
        out_ref[index] = (scale * sums[index]).astype(jnp.bfloat16)
        return carry

    lax.fori_loop(0, rows, finish, 0)


def per_device(
    tokens,
    grad_out,
    packed_weight_blocks,
    packed_first_moments,
    packed_second_moments,
    block_mask,
    last_step,
    regrown,
    step_now,
):
    scale_factor = 3.0 / math.sqrt(D)
    tok_count = tokens.shape[0]
    owned_slots = packed_weight_blocks.shape[0]
    block_size = packed_weight_blocks.shape[1]
    row_blocks = block_mask.shape[1]
    column_blocks = block_mask.shape[2]
    local_rows = tokens.shape[1] // block_size
    groups = lax.axis_size("dp")
    slot_total = owned_slots * groups
    step_value = step_now[0]
    own_left = jnp.concatenate(
        [
            tokens.reshape(tok_count, local_rows, block_size),
            grad_out.reshape(tok_count, local_rows, block_size),
        ],
        axis=1,
    ).transpose(1, 0, 2)
    own_packed = packed_weight_blocks.astype(jnp.bfloat16)
    packed, left_source = gather_all(own_packed, own_left)
    _, block_index, slot_regrown, slot_last, live_count = slot_table(
        block_mask, regrown, last_step, slot_total
    )
    matrix_of = block_index // (row_blocks * column_blocks)
    row_of = block_index // column_blocks % row_blocks
    column_of = block_index % column_blocks
    slot_ids = jnp.arange(slot_total, dtype=jnp.int32)
    usable = (slot_ids < live_count) & (slot_regrown == 0)
    left_at = (row_of // local_rows * 2 + matrix_of) * local_rows + row_of % local_rows
    right_at = matrix_of * column_blocks + column_of
    sum_at = jnp.where(usable, right_at, 2 * column_blocks)
    row_at = jnp.where(usable & (matrix_of == 0), row_of, row_blocks)
    up_count = jnp.sum(block_mask[0], dtype=jnp.int32)
    up_steps = ((up_count + UNROLL - 1) // UNROLL).reshape(1)
    smem = pl.BlockSpec(memory_space=pltpu.SMEM)
    vmem = pl.BlockSpec(memory_space=pltpu.VMEM)
    params = pltpu.CompilerParams(vmem_limit_bytes=48 * 1024 * 1024)
    block = (tok_count, block_size)
    right_source, tiles = pl.pallas_call(
        functools.partial(forward_kernel, scale=scale_factor),
        out_shape=(
            jax.ShapeDtypeStruct((2 * column_blocks,) + block, jnp.bfloat16),
            jax.ShapeDtypeStruct((slot_total, block_size, block_size), jnp.bfloat16),
        ),
        in_specs=[smem] * 3 + [vmem] * 2,
        out_specs=(vmem, vmem),
        scratch_shapes=[pltpu.VMEM((2 * column_blocks + 1,) + block, jnp.float32)],
        compiler_params=params,
    )(left_at, right_at, sum_at, packed, left_source)
    partial_rows = pl.pallas_call(
        functools.partial(input_grad_kernel, scale=scale_factor),
        out_shape=jax.ShapeDtypeStruct((row_blocks,) + block, jnp.bfloat16),
        in_specs=[smem] * 3 + [vmem] * 2,
        out_specs=vmem,
        scratch_shapes=[pltpu.VMEM((row_blocks + 1,) + block, jnp.float32)],
        compiler_params=params,
    )(right_at, row_at, up_steps, packed, right_source)
    block_grads, summed_rows = reduce_all(tiles, partial_rows)
    input_grad = (
        summed_rows.transpose(1, 0, 2).reshape(tok_count, tokens.shape[1]).astype(jnp.bfloat16)
    )
    owner_first = lax.axis_index("dp") * owned_slots
    mine_regrown = lax.dynamic_slice_in_dim(slot_regrown, owner_first, owned_slots)
    mine_last = lax.dynamic_slice_in_dim(slot_last, owner_first, owned_slots)
    live_slots = owner_first + jnp.arange(owned_slots, dtype=jnp.int32) < live_count
    new_weights, new_first, new_second = adam_step(
        packed_weight_blocks,
        packed_first_moments,
        packed_second_moments,
        block_grads,
        live_slots,
        mine_regrown,
        mine_last,
        step_value,
    )
    return (input_grad, new_weights, new_first, new_second)


def solution(mesh):
    in_specs = (
        P("dp", "tensor"),
        P("dp", "tensor"),
        P(("dp", "tensor"), None, None),
        P(("dp", "tensor"), None, None),
        P(("dp", "tensor"), None, None),
        P(None, None, "tensor"),
        P(None, None, "tensor"),
        P(None, None, "tensor"),
        P(),
    )
    out_specs = (
        P("dp", "tensor"),
        P(("dp", "tensor"), None, None),
        P(("dp", "tensor"), None, None),
        P(("dp", "tensor"), None, None),
    )
    return jax.shard_map(
        per_device, mesh=mesh, in_specs=in_specs, out_specs=out_specs, check_vma=False
    )
```

```python
import functools
import math

import jax
import jax.numpy as jnp
from jax import lax
from jax.experimental import pallas as pl
from jax.experimental.pallas import tpu as pltpu
from jax.sharding import PartitionSpec as P

D = 8192


beta_one = 0.9
beta_two = 0.95
learn_rate = 0.05
decay_rate = 0.1
epsilon = 0.05


def silu_slope(values):
    sigmoid = jax.nn.sigmoid(values)
    return sigmoid * (1.0 + values * (1.0 - sigmoid))


def slot_table(mask_grid, regrown_grid, last_grid, slot_total):
    flags = mask_grid.reshape(-1)
    numbered = jnp.cumsum(flags, dtype=jnp.int32) - 1
    block_total = flags.shape[0]
    matches = (numbered[None, :] == jnp.arange(slot_total, dtype=jnp.int32)[:, None]) & (
        flags[None, :] == 1
    )
    block_index = jnp.sum(
        jnp.where(matches, jnp.arange(block_total, dtype=jnp.int32)[None, :], 0),
        axis=1,
        dtype=jnp.int32,
    )
    slot_regrown = jnp.sum(
        jnp.where(matches, regrown_grid.reshape(-1)[None, :], 0), axis=1, dtype=jnp.int32
    )
    slot_last = jnp.sum(
        jnp.where(matches, last_grid.reshape(-1)[None, :], 0), axis=1, dtype=jnp.int32
    )
    live_count = jnp.sum(flags, dtype=jnp.int32)
    return (numbered, block_index, slot_regrown, slot_last, live_count)


def adam_step(
    weights, first_in, second_in, block_grads, live_slots, slot_regrown, slot_last, step_value
):
    regrown_now = (slot_regrown == 1)[:, None, None]
    skipped = (step_value - slot_last - 1).astype(jnp.float32)[:, None, None]
    base_weight = jnp.where(regrown_now, jnp.float32(0.0), weights)
    kept_first = jnp.where(
        regrown_now, jnp.float32(0.0), first_in * jnp.power(jnp.float32(beta_one), skipped)
    )
    kept_second = jnp.where(
        regrown_now, jnp.float32(0.0), second_in * jnp.power(jnp.float32(beta_two), skipped)
    )
    new_first = beta_one * kept_first + (1.0 - beta_one) * block_grads
    new_second = beta_two * kept_second + (1.0 - beta_two) * block_grads * block_grads
    bias_count = jnp.where(
        regrown_now, jnp.float32(1.0), step_value.astype(jnp.float32) + jnp.zeros_like(skipped)
    )
    first_hat = new_first / (1.0 - jnp.power(jnp.float32(beta_one), bias_count))
    second_hat = new_second / (1.0 - jnp.power(jnp.float32(beta_two), bias_count))
    new_weight = base_weight - learn_rate * (
        first_hat / (jnp.sqrt(second_hat) + epsilon) + decay_rate * base_weight
    )
    keep_slot = live_slots[:, None, None]
    return (
        jnp.where(keep_slot, new_weight, weights),
        jnp.where(keep_slot, new_first, first_in),
        jnp.where(keep_slot, new_second, second_in),
    )


INNER = 2


def piece(index, chunk, chunks, shard):
    size = shard // chunks
    return pl.ds((index * chunks + chunk) * size, size)


def remote(src, dst, send_sem, recv_sem, axis, target):
    return pltpu.make_async_remote_copy(
        src_ref=src,
        dst_ref=dst,
        send_sem=send_sem,
        recv_sem=recv_sem,
        device_id={axis: target},
        device_id_type=pl.DeviceIdType.MESH,
    )


def greet(targets):
    barrier = pltpu.get_barrier_semaphore()
    for axis, target, exists in targets:

        @pl.when(exists)
        def _(axis=axis, target=target):
            pl.semaphore_signal(
                barrier, inc=1, device_id={axis: target}, device_id_type=pl.DeviceIdType.MESH
            )

    pl.semaphore_wait(barrier, sum(jnp.where(exists, 1, 0) for _, _, exists in targets))


class LineGather:
    def __init__(self, axis, size, chunks, own, out, sems):
        self.axis, self.chunks, self.own, self.out = axis, chunks, own, out
        self.recv, self.up, self.down, self.across, self.local = sems
        self.outer = size // INNER
        me = lax.axis_index(axis)
        self.me, self.mine, self.inner = me, me // INNER, me % INNER
        self.shard = own.shape[0]

    def targets(self):
        mine = self.mine
        return [
            (self.axis, self.me + INNER, mine + 1 < self.outer),
            (self.axis, self.me - INNER, mine > 0),
            (self.axis, mine * INNER + 1 - self.inner, mine >= 0),
        ]

    def copy(self, source, chunk, way, inner=None):
        inner = self.inner if inner is None else inner
        index = source * INNER + inner
        at = self.out.at[piece(index, chunk, self.chunks, self.shard)]
        slot = source * self.chunks + chunk
        sem, target = {
            "up": (self.up, self.me + INNER),
            "down": (self.down, self.me - INNER),
            "across": (self.across, self.mine * INNER + 1 - self.inner),
        }[way]
        recv = self.recv.at[index * self.chunks + chunk]
        return at, sem.at[slot], recv, target

    def send(self, source, chunk, way, own=False):
        at, sem, recv, target = self.copy(source, chunk, way)
        src = self.own.at[piece(0, chunk, self.chunks, self.shard)] if own else at
        remote(src, at, sem, recv, self.axis, target).start()

    def wait_send(self, source, chunk, way):
        at, sem, recv, target = self.copy(source, chunk, way)
        remote(at, at, sem, recv, self.axis, target).wait_send()

    def wait_recv(self, source, chunk, inner):
        at, sem, recv, target = self.copy(source, chunk, "across", inner)
        remote(at, at, sem, recv, self.axis, target).wait_recv()

    def own_copy(self):
        at = self.out.at[pl.ds(self.me * self.shard, self.shard)]
        return pltpu.make_async_copy(self.own, at, self.local)

    def begin(self, chunk):
        mine = self.mine

        @pl.when(mine + 1 < self.outer)
        def _():
            self.send(mine, chunk, "up", own=True)

        @pl.when(mine > 0)
        def _():
            self.send(mine, chunk, "down", own=True)

        self.send(mine, chunk, "across", own=True)

    def step(self, distance, chunk):
        low, high = self.mine - distance, self.mine + distance

        @pl.when(low >= 0)
        def _():
            self.wait_recv(low, chunk, self.inner)

            @pl.when(self.mine + 1 < self.outer)
            def _():
                self.send(low, chunk, "up")

            self.send(low, chunk, "across")

        @pl.when(high < self.outer)
        def _():
            self.wait_recv(high, chunk, self.inner)

            @pl.when(self.mine > 0)
            def _():
                self.send(high, chunk, "down")

            self.send(high, chunk, "across")

    def finish(self):
        for source in range(self.outer):
            for chunk in range(self.chunks):
                self.wait_recv(source, chunk, 1 - self.inner)
                self.wait_send(source, chunk, "across")

                @pl.when((self.mine >= source) & (self.mine + 1 < self.outer))
                def _(source=source, chunk=chunk):
                    self.wait_send(source, chunk, "up")

                @pl.when((self.mine <= source) & (self.mine > 0))
                def _(source=source, chunk=chunk):
                    self.wait_send(source, chunk, "down")

        self.own_copy().wait()


def gather_kernel(sizes, chunk_counts, own_packed, own_left, packed_out, left_out, *sems):
    lines = [
        LineGather("dp", sizes[0], chunk_counts[0], own_packed, packed_out, sems[:5]),
        LineGather("tensor", sizes[1], chunk_counts[1], own_left, left_out, sems[5:]),
    ]
    greet(lines[0].targets() + lines[1].targets())
    events = []
    for line in lines:
        for chunk in range(line.chunks):
            events.append((chunk / line.chunks, line, 0, chunk))
            for distance in range(1, line.outer):
                when = 1 + (distance - 1 + (chunk + 1) / line.chunks) / (line.outer - 1)
                events.append((when, line, distance, chunk))
    events.sort(key=lambda event: event[0])
    for when, line, distance, chunk in events:
        if distance == 0:
            line.begin(chunk)
    for line in lines:
        line.own_copy().start()
    for when, line, distance, chunk in events:
        if distance > 0:
            line.step(distance, chunk)
    for line in lines:
        line.finish()


def line_sems(size, chunks):
    dma = pltpu.SemaphoreType.DMA
    outer = size // INNER
    return [dma((size * chunks,))] + [dma((outer * chunks,))] * 3 + [dma]


def gather_all(own_packed, own_left):
    sizes = (lax.axis_size("dp"), lax.axis_size("tensor"))
    chunk_counts = (math.gcd(4, own_packed.shape[0]), math.gcd(2, own_left.shape[0]))
    vmem = pl.BlockSpec(memory_space=pltpu.VMEM)
    return pl.pallas_call(
        functools.partial(gather_kernel, sizes, chunk_counts),
        out_shape=(
            jax.ShapeDtypeStruct((sizes[0] * own_packed.shape[0],) + own_packed.shape[1:], jnp.bfloat16),
            jax.ShapeDtypeStruct((sizes[1] * own_left.shape[0],) + own_left.shape[1:], jnp.bfloat16),
        ),
        in_specs=[vmem, vmem],
        out_specs=(pl.BlockSpec(memory_space=pl.ANY), pl.BlockSpec(memory_space=pl.ANY)),
        scratch_shapes=line_sems(sizes[0], chunk_counts[0]) + line_sems(sizes[1], chunk_counts[1]),
        compiler_params=pltpu.CompilerParams(
            collective_id=0, has_side_effects=True, vmem_limit_bytes=48 * 1024 * 1024
        ),
    )(own_packed, own_left)


class PairReduce:
    def __init__(self, axis, size, chunks, data, out, near, far, sems):
        self.axis, self.chunks, self.data, self.out = axis, chunks, data, out
        self.near, self.far = near, far
        self.near_send, self.near_recv, self.far_send, self.far_recv = sems
        self.outer = size // INNER
        me = lax.axis_index(axis)
        self.me, self.mine, self.inner = me, me // INNER, me % INNER
        self.shard = out.shape[0]

    def owner(self, offset):
        return lax.rem(self.mine + offset, self.outer)

    def targets(self):
        far = [
            (self.axis, self.owner(offset) * INNER + self.inner, self.mine >= 0)
            for offset in range(1, self.outer)
        ]
        return far + [(self.axis, self.mine * INNER + 1 - self.inner, self.mine >= 0)]

    def near_copy(self, offset, chunk):
        owner = self.owner(offset)
        other = 1 - self.inner
        slot = owner * self.chunks + chunk
        return remote(
            self.data.at[piece(owner * INNER + other, chunk, self.chunks, self.shard)],
            self.near.at[piece(owner, chunk, self.chunks, self.shard)],
            self.near_send.at[slot],
            self.near_recv.at[slot],
            self.axis,
            self.mine * INNER + other,
        )

    def far_copy(self, offset, chunk):
        owner = self.owner(offset)
        return remote(
            self.near.at[piece(owner, chunk, self.chunks, self.shard)],
            self.far.at[piece(offset - 1, chunk, self.chunks, self.shard)],
            self.far_send.at[(offset - 1) * self.chunks + chunk],
            self.far_recv.at[(offset - 1) * self.chunks + chunk],
            self.axis,
            owner * INNER + self.inner,
        )

    def send_pair(self, offset, chunk):
        self.near_copy(offset, chunk).wait_recv()
        owner = self.owner(offset)
        size = self.shard // self.chunks
        near_at = (owner * self.chunks + chunk) * size
        data_at = ((owner * INNER + self.inner) * self.chunks + chunk) * size

        def add(index, carry):
            total = self.near[near_at + index].astype(jnp.float32)
            total += self.data[data_at + index].astype(jnp.float32)
            self.near[near_at + index] = total.astype(jnp.bfloat16)
            return carry

        lax.fori_loop(0, size, add, 0)
        self.far_copy(offset, chunk).start()

    def total(self, chunk):
        self.near_copy(0, chunk).wait_recv()
        for offset in range(1, self.outer):
            self.far_copy(offset, chunk).wait_recv()
        size = self.shard // self.chunks
        near_at = (self.mine * self.chunks + chunk) * size
        data_at = (self.me * self.chunks + chunk) * size

        def add(index, carry):
            total = self.near[near_at + index].astype(jnp.float32)
            total += self.data[data_at + index].astype(jnp.float32)
            for offset in range(1, self.outer):
                at = ((offset - 1) * self.chunks + chunk) * size
                total += self.far[at + index].astype(jnp.float32)
            self.out[chunk * size + index] = total.astype(self.out.dtype)
            return carry

        lax.fori_loop(0, size, add, 0)

    def finish(self):
        for chunk in range(self.chunks):
            for offset in range(self.outer):
                self.near_copy(offset, chunk).wait_send()
                if offset > 0:
                    self.far_copy(offset, chunk).wait_send()


def make_tiles(left_at, right_at, left_ref, right_ref, tiles_ref, first, count, scale):
    unroll = math.gcd(UNROLL, count)

    def step(index, carry):
        base = first + index * unroll
        for k in range(unroll):
            tile = lax.dot_general(
                left_ref[left_at[base + k]],
                right_ref[right_at[base + k]],
                (((0,), (0,)), ((), ())),
                preferred_element_type=jnp.float32,
            )
            tiles_ref[base + k] = (scale * tile).astype(jnp.bfloat16)
        return carry

    lax.fori_loop(0, count // unroll, step, 0)


def reduce_kernel(
    sizes,
    chunk_counts,
    scale,
    left_at,
    right_at,
    left_ref,
    right_ref,
    rows,
    grads_out,
    rows_out,
    tiles,
    *scratch,
):
    wide = PairReduce(
        "dp", sizes[0], chunk_counts[0], tiles, grads_out, scratch[0], scratch[1], scratch[4:8]
    )
    thin = PairReduce(
        "tensor", sizes[1], chunk_counts[1], rows, rows_out, scratch[2], scratch[3], scratch[8:]
    )
    greet(wide.targets() + thin.targets())
    for offset in list(range(1, thin.outer)) + [0]:
        for chunk in range(thin.chunks):
            thin.near_copy(offset, chunk).start()
    size = wide.shard // wide.chunks
    thin_pairs = [(o, k) for o in range(1, thin.outer) for k in range(thin.chunks)]
    wide_steps = [(o, k) for o in list(range(1, wide.outer)) + [0] for k in range(wide.chunks)]
    for at, (offset, chunk) in enumerate(wide_steps):
        owner = wide.owner(offset)
        for inner in (1 - wide.inner, wide.inner):
            first = ((owner * INNER + inner) * wide.chunks + chunk) * size
            make_tiles(left_at, right_at, left_ref, right_ref, tiles, first, size, scale)
            if inner is not wide.inner:
                wide.near_copy(offset, chunk).start()
        if offset > 0:
            wide.send_pair(offset, chunk)
        low = at * len(thin_pairs) // len(wide_steps)
        high = (at + 1) * len(thin_pairs) // len(wide_steps)
        for pair in thin_pairs[low:high]:
            thin.send_pair(*pair)
    for chunk in range(wide.chunks - 1):
        wide.total(chunk)
    for chunk in range(thin.chunks):
        thin.total(chunk)
    wide.total(wide.chunks - 1)
    wide.finish()
    thin.finish()


def pair_sems(size, chunks):
    dma = pltpu.SemaphoreType.DMA
    outer = size // INNER
    return [dma((outer * chunks,))] * 2 + [dma((max(outer - 1, 1) * chunks,))] * 2


def reduce_all(left_at, right_at, left_source, right_source, partial_rows, scale):
    sizes = (lax.axis_size("dp"), lax.axis_size("tensor"))
    side = left_source.shape[2]
    tile_shape = (left_at.shape[0], side, side)
    shards = (tile_shape[0] // sizes[0], partial_rows.shape[0] // sizes[1])
    chunk_counts = (math.gcd(4, shards[0]), math.gcd(2, shards[1]))
    vmem = pl.BlockSpec(memory_space=pltpu.VMEM)
    smem = pl.BlockSpec(memory_space=pltpu.SMEM)
    scratch = [pltpu.VMEM(tile_shape, jnp.bfloat16)]
    for shape, size, shard in zip((tile_shape, partial_rows.shape), sizes, shards):
        outer = size // INNER
        scratch.append(pltpu.VMEM((outer * shard,) + shape[1:], jnp.bfloat16))
        scratch.append(pltpu.VMEM((max(outer - 1, 1) * shard,) + shape[1:], jnp.bfloat16))
    return pl.pallas_call(
        functools.partial(reduce_kernel, sizes, chunk_counts, scale),
        out_shape=(
            jax.ShapeDtypeStruct((shards[0],) + tile_shape[1:], jnp.float32),
            jax.ShapeDtypeStruct((shards[1],) + partial_rows.shape[1:], jnp.bfloat16),
        ),
        in_specs=[smem, smem, vmem, vmem, vmem],
        out_specs=(vmem, vmem),
        scratch_shapes=scratch
        + pair_sems(sizes[0], chunk_counts[0])
        + pair_sems(sizes[1], chunk_counts[1]),
        compiler_params=pltpu.CompilerParams(
            collective_id=1, has_side_effects=True, vmem_limit_bytes=48 * 1024 * 1024
        ),
    )(left_at, right_at, left_source, right_source, partial_rows)


UNROLL = 4


def forward_kernel(
    left_at,
    right_at,
    sum_at,
    row_at,
    up_steps,
    packed_ref,
    left_ref,
    right_ref,
    out_ref,
    sums,
    row_sums,
    *,
    scale,
):
    slot_total = packed_ref.shape[0]
    columns = right_ref.shape[0] // 2

    def clear(index, carry):
        sums[index] = jnp.zeros(sums.shape[1:], jnp.float32)
        return carry

    lax.fori_loop(0, sums.shape[0], clear, 0)

    def add_slots(step, carry):
        base = step * UNROLL
        parts = [
            jnp.dot(
                left_ref[left_at[base + k]],
                packed_ref[base + k],
                preferred_element_type=jnp.float32,
            )
            for k in range(UNROLL)
        ]
        for k in range(UNROLL):
            sums[sum_at[base + k]] += parts[k]
        return carry

    lax.fori_loop(0, slot_total // UNROLL, add_slots, 0)

    def activate(column, carry):
        pre_act = scale * sums[column]
        back_act = scale * sums[columns + column]
        right_ref[column] = (back_act * silu_slope(pre_act)).astype(jnp.bfloat16)
        right_ref[columns + column] = jax.nn.silu(pre_act).astype(jnp.bfloat16)
        return carry

    lax.fori_loop(0, columns, activate, 0)

    add_input_grad(right_at, row_at, up_steps, packed_ref, right_ref, out_ref, row_sums, scale)


def add_input_grad(right_at, row_at, up_steps, packed_ref, right_ref, out_ref, sums, scale):
    rows = out_ref.shape[0]

    def clear(index, carry):
        sums[index] = jnp.zeros(sums.shape[1:], jnp.float32)
        return carry

    lax.fori_loop(0, rows, clear, 0)

    def add_slots(step, carry):
        base = step * UNROLL
        parts = [
            lax.dot_general(
                right_ref[right_at[base + k]],
                packed_ref[base + k],
                (((1,), (1,)), ((), ())),
                preferred_element_type=jnp.float32,
            )
            for k in range(UNROLL)
        ]
        for k in range(UNROLL):
            sums[row_at[base + k]] += parts[k]
        return carry

    lax.fori_loop(0, up_steps[0], add_slots, 0)

    def finish(index, carry):
        out_ref[index] = (scale * sums[index]).astype(jnp.bfloat16)
        return carry

    lax.fori_loop(0, rows, finish, 0)


def per_device(
    tokens,
    grad_out,
    packed_weight_blocks,
    packed_first_moments,
    packed_second_moments,
    block_mask,
    last_step,
    regrown,
    step_now,
):
    scale_factor = 3.0 / math.sqrt(D)
    tok_count = tokens.shape[0]
    owned_slots = packed_weight_blocks.shape[0]
    block_size = packed_weight_blocks.shape[1]
    row_blocks = block_mask.shape[1]
    column_blocks = block_mask.shape[2]
    local_rows = tokens.shape[1] // block_size
    groups = lax.axis_size("dp")
    slot_total = owned_slots * groups
    step_value = step_now[0]
    own_left = jnp.concatenate(
        [
            tokens.reshape(tok_count, local_rows, block_size),
            grad_out.reshape(tok_count, local_rows, block_size),
        ],
        axis=1,
    ).transpose(1, 0, 2)
    own_packed = packed_weight_blocks.astype(jnp.bfloat16)
    packed, left_source = gather_all(own_packed, own_left)
    _, block_index, slot_regrown, slot_last, live_count = slot_table(
        block_mask, regrown, last_step, slot_total
    )
    matrix_of = block_index // (row_blocks * column_blocks)
    row_of = block_index // column_blocks % row_blocks
    column_of = block_index % column_blocks
    slot_ids = jnp.arange(slot_total, dtype=jnp.int32)
    usable = (slot_ids < live_count) & (slot_regrown == 0)
    left_at = (row_of // local_rows * 2 + matrix_of) * local_rows + row_of % local_rows
    right_at = matrix_of * column_blocks + column_of
    sum_at = jnp.where(usable, right_at, 2 * column_blocks)
    row_at = jnp.where(usable & (matrix_of == 0), row_of, row_blocks)
    up_count = jnp.sum(block_mask[0], dtype=jnp.int32)
    up_steps = ((up_count + UNROLL - 1) // UNROLL).reshape(1)
    smem = pl.BlockSpec(memory_space=pltpu.SMEM)
    vmem = pl.BlockSpec(memory_space=pltpu.VMEM)
    params = pltpu.CompilerParams(vmem_limit_bytes=48 * 1024 * 1024)
    block = (tok_count, block_size)
    right_source, partial_rows = pl.pallas_call(
        functools.partial(forward_kernel, scale=scale_factor),
        out_shape=(
            jax.ShapeDtypeStruct((2 * column_blocks,) + block, jnp.bfloat16),
            jax.ShapeDtypeStruct((row_blocks,) + block, jnp.bfloat16),
        ),
        in_specs=[smem] * 5 + [vmem] * 2,
        out_specs=(vmem, vmem),
        scratch_shapes=[
            pltpu.VMEM((2 * column_blocks + 1,) + block, jnp.float32),
            pltpu.VMEM((row_blocks + 1,) + block, jnp.float32),
        ],
        compiler_params=params,
    )(left_at, right_at, sum_at, row_at, up_steps, packed, left_source)
    block_grads, summed_rows = reduce_all(
        left_at, right_at, left_source, right_source, partial_rows, scale_factor
    )
    input_grad = (
        summed_rows.transpose(1, 0, 2).reshape(tok_count, tokens.shape[1]).astype(jnp.bfloat16)
    )
    owner_first = lax.axis_index("dp") * owned_slots
    mine_regrown = lax.dynamic_slice_in_dim(slot_regrown, owner_first, owned_slots)
    mine_last = lax.dynamic_slice_in_dim(slot_last, owner_first, owned_slots)
    live_slots = owner_first + jnp.arange(owned_slots, dtype=jnp.int32) < live_count
    new_weights, new_first, new_second = adam_step(
        packed_weight_blocks,
        packed_first_moments,
        packed_second_moments,
        block_grads,
        live_slots,
        mine_regrown,
        mine_last,
        step_value,
    )
    return (input_grad, new_weights, new_first, new_second)


def solution(mesh):
    in_specs = (
        P("dp", "tensor"),
        P("dp", "tensor"),
        P(("dp", "tensor"), None, None),
        P(("dp", "tensor"), None, None),
        P(("dp", "tensor"), None, None),
        P(None, None, "tensor"),
        P(None, None, "tensor"),
        P(None, None, "tensor"),
        P(),
    )
    out_specs = (
        P("dp", "tensor"),
        P(("dp", "tensor"), None, None),
        P(("dp", "tensor"), None, None),
        P(("dp", "tensor"), None, None),
    )
    return jax.shard_map(
        per_device, mesh=mesh, in_specs=in_specs, out_specs=out_specs, check_vma=False
    )
```

```python
import functools
import math

import jax
import jax.numpy as jnp
from jax import lax
from jax.experimental import pallas as pl
from jax.experimental.pallas import tpu as pltpu
from jax.sharding import PartitionSpec as P

D = 8192


beta_one = 0.9
beta_two = 0.95
learn_rate = 0.05
decay_rate = 0.1
epsilon = 0.05


def silu_slope(values):
    sigmoid = jax.nn.sigmoid(values)
    return sigmoid * (1.0 + values * (1.0 - sigmoid))


def slot_table(mask_grid, regrown_grid, last_grid, slot_total):
    codes = lax.optimization_barrier((mask_grid + 2 * regrown_grid + 4 * last_grid).reshape(-1))
    flags = codes & 1
    numbered = jnp.cumsum(flags, dtype=jnp.int32) - 1
    block_total = flags.shape[0]
    wanted = jnp.where(flags == 1, numbered, -1)
    entries = jnp.arange(block_total, dtype=jnp.int32) + block_total * (codes >> 1)
    matches = wanted[None, :] == jnp.arange(slot_total, dtype=jnp.int32)[:, None]
    found = lax.optimization_barrier(
        jnp.sum(jnp.where(matches, entries[None, :], 0), axis=1, dtype=jnp.int32)
    )
    block_index = found % block_total
    slot_regrown = found // block_total & 1
    slot_last = found // block_total // 2
    live_count = jnp.sum(flags, dtype=jnp.int32)
    up_count = jnp.sum(flags[: block_total // 2], dtype=jnp.int32)
    return (block_index, slot_regrown, slot_last, live_count, up_count)


def adam_step(
    weights, first_in, second_in, block_grads, live_slots, slot_regrown, slot_last, step_value
):
    regrown_now = (slot_regrown == 1)[:, None, None]
    skipped = (step_value - slot_last - 1).astype(jnp.float32)[:, None, None]
    base_weight = jnp.where(regrown_now, jnp.float32(0.0), weights)
    kept_first = jnp.where(
        regrown_now, jnp.float32(0.0), first_in * jnp.power(jnp.float32(beta_one), skipped)
    )
    kept_second = jnp.where(
        regrown_now, jnp.float32(0.0), second_in * jnp.power(jnp.float32(beta_two), skipped)
    )
    new_first = beta_one * kept_first + (1.0 - beta_one) * block_grads
    new_second = beta_two * kept_second + (1.0 - beta_two) * block_grads * block_grads
    bias_count = jnp.where(
        regrown_now, jnp.float32(1.0), step_value.astype(jnp.float32) + jnp.zeros_like(skipped)
    )
    first_hat = new_first / (1.0 - jnp.power(jnp.float32(beta_one), bias_count))
    second_hat = new_second / (1.0 - jnp.power(jnp.float32(beta_two), bias_count))
    new_weight = base_weight - learn_rate * (
        first_hat / (jnp.sqrt(second_hat) + epsilon) + decay_rate * base_weight
    )
    keep_slot = live_slots[:, None, None]
    return (
        jnp.where(keep_slot, new_weight, weights),
        jnp.where(keep_slot, new_first, first_in),
        jnp.where(keep_slot, new_second, second_in),
    )


INNER = 2


def piece(index, chunk, chunks, shard):
    size = shard // chunks
    return pl.ds((index * chunks + chunk) * size, size)


def remote(src, dst, send_sem, recv_sem, axis, target):
    return pltpu.make_async_remote_copy(
        src_ref=src,
        dst_ref=dst,
        send_sem=send_sem,
        recv_sem=recv_sem,
        device_id={axis: target},
        device_id_type=pl.DeviceIdType.MESH,
    )


def greet(targets, meanwhile=None):
    barrier = pltpu.get_barrier_semaphore()
    for axis, target, exists in targets:

        @pl.when(exists)
        def _(axis=axis, target=target):
            pl.semaphore_signal(
                barrier, inc=1, device_id={axis: target}, device_id_type=pl.DeviceIdType.MESH
            )

    if meanwhile is not None:
        meanwhile()
    pl.semaphore_wait(barrier, sum(jnp.where(exists, 1, 0) for _, _, exists in targets))


class LineGather:
    def __init__(self, axis, size, chunks, own, out, sems):
        self.axis, self.chunks, self.own, self.out = axis, chunks, own, out
        self.recv, self.up, self.down, self.across, self.local = sems
        self.outer = size // INNER
        me = lax.axis_index(axis)
        self.me, self.mine, self.inner = me, me // INNER, me % INNER
        self.shard = own.shape[0]

    def targets(self):
        mine = self.mine
        return [
            (self.axis, self.me + INNER, mine + 1 < self.outer),
            (self.axis, self.me - INNER, mine > 0),
            (self.axis, mine * INNER + 1 - self.inner, mine >= 0),
        ]

    def copy(self, source, chunk, way, inner=None):
        inner = self.inner if inner is None else inner
        index = source * INNER + inner
        at = self.out.at[piece(index, chunk, self.chunks, self.shard)]
        slot = source * self.chunks + chunk
        sem, target = {
            "up": (self.up, self.me + INNER),
            "down": (self.down, self.me - INNER),
            "across": (self.across, self.mine * INNER + 1 - self.inner),
        }[way]
        recv = self.recv.at[index * self.chunks + chunk]
        return at, sem.at[slot], recv, target

    def send(self, source, chunk, way, own=False):
        at, sem, recv, target = self.copy(source, chunk, way)
        src = self.own.at[piece(0, chunk, self.chunks, self.shard)] if own else at
        remote(src, at, sem, recv, self.axis, target).start()

    def wait_send(self, source, chunk, way):
        at, sem, recv, target = self.copy(source, chunk, way)
        remote(at, at, sem, recv, self.axis, target).wait_send()

    def wait_recv(self, source, chunk, inner):
        at, sem, recv, target = self.copy(source, chunk, "across", inner)
        remote(at, at, sem, recv, self.axis, target).wait_recv()

    def own_copy(self):
        at = self.out.at[pl.ds(self.me * self.shard, self.shard)]
        return pltpu.make_async_copy(self.own, at, self.local)

    def begin(self, chunk):
        mine = self.mine

        @pl.when(mine + 1 < self.outer)
        def _():
            self.send(mine, chunk, "up", own=True)

        @pl.when(mine > 0)
        def _():
            self.send(mine, chunk, "down", own=True)

        self.send(mine, chunk, "across", own=True)

    def step(self, distance, chunk):
        low, high = self.mine - distance, self.mine + distance

        @pl.when(low >= 0)
        def _():
            self.wait_recv(low, chunk, self.inner)

            @pl.when(self.mine + 1 < self.outer)
            def _():
                self.send(low, chunk, "up")

            self.send(low, chunk, "across")

        @pl.when(high < self.outer)
        def _():
            self.wait_recv(high, chunk, self.inner)

            @pl.when(self.mine > 0)
            def _():
                self.send(high, chunk, "down")

            self.send(high, chunk, "across")

    def finish(self):
        for source in range(self.outer):
            for chunk in range(self.chunks):
                self.wait_recv(source, chunk, 1 - self.inner)
                self.wait_send(source, chunk, "across")

                @pl.when((self.mine >= source) & (self.mine + 1 < self.outer))
                def _(source=source, chunk=chunk):
                    self.wait_send(source, chunk, "up")

                @pl.when((self.mine <= source) & (self.mine > 0))
                def _(source=source, chunk=chunk):
                    self.wait_send(source, chunk, "down")

        self.own_copy().wait()


def gather_kernel(
    sizes,
    chunk_counts,
    weights,
    tokens,
    grad_out,
    packed_out,
    left_out,
    own_packed,
    own_left,
    *sems,
):
    lines = [
        LineGather("dp", sizes[0], chunk_counts[0], own_packed, packed_out, sems[:5]),
        LineGather("tensor", sizes[1], chunk_counts[1], own_left, left_out, sems[5:]),
    ]

    def round_own():
        side = own_left.shape[2]
        local_rows = own_left.shape[0] // 2
        for row in range(local_rows):
            own_left[row] = tokens[:, row * side : (row + 1) * side]
            own_left[local_rows + row] = grad_out[:, row * side : (row + 1) * side]

        def round_block(index, carry):
            own_packed[index] = weights[index].astype(jnp.bfloat16)
            return carry

        lax.fori_loop(0, own_packed.shape[0], round_block, 0)

    greet(lines[0].targets() + lines[1].targets(), round_own)
    events = []
    for line in lines:
        for chunk in range(line.chunks):
            events.append((chunk / line.chunks, line, 0, chunk))
            for distance in range(1, line.outer):
                when = 1 + (distance - 1 + (chunk + 1) / line.chunks) / (line.outer - 1)
                events.append((when, line, distance, chunk))
    events.sort(key=lambda event: event[0])
    for when, line, distance, chunk in events:
        if distance == 0:
            line.begin(chunk)
    for line in lines:
        line.own_copy().start()
    for when, line, distance, chunk in events:
        if distance > 0:
            line.step(distance, chunk)
    for line in lines:
        line.finish()


def line_sems(size, chunks):
    dma = pltpu.SemaphoreType.DMA
    outer = size // INNER
    return [dma((size * chunks,))] + [dma((outer * chunks,))] * 3 + [dma]


def gather_all(weights, tokens, grad_out):
    sizes = (lax.axis_size("dp"), lax.axis_size("tensor"))
    side = weights.shape[1]
    own_left = (2 * tokens.shape[1] // side, tokens.shape[0], side)
    chunk_counts = (math.gcd(4, weights.shape[0]), math.gcd(2, own_left[0]))
    vmem = pl.BlockSpec(memory_space=pltpu.VMEM)
    anywhere = pl.BlockSpec(memory_space=pl.ANY)
    return pl.pallas_call(
        functools.partial(gather_kernel, sizes, chunk_counts),
        out_shape=(
            jax.ShapeDtypeStruct((sizes[0] * weights.shape[0], side, side), jnp.bfloat16),
            jax.ShapeDtypeStruct((sizes[1] * own_left[0],) + own_left[1:], jnp.bfloat16),
        ),
        in_specs=[vmem, vmem, vmem],
        out_specs=(anywhere, anywhere),
        scratch_shapes=[
            pltpu.VMEM(weights.shape, jnp.bfloat16),
            pltpu.VMEM(own_left, jnp.bfloat16),
        ]
        + line_sems(sizes[0], chunk_counts[0])
        + line_sems(sizes[1], chunk_counts[1]),
        compiler_params=pltpu.CompilerParams(
            collective_id=0, has_side_effects=True, vmem_limit_bytes=48 * 1024 * 1024
        ),
    )(weights, tokens, grad_out)


class PairReduce:
    def __init__(self, axis, size, chunks, data, out, near, far, sems):
        self.axis, self.chunks, self.data, self.out = axis, chunks, data, out
        self.near, self.far = near, far
        self.near_send, self.near_recv, self.far_send, self.far_recv = sems
        self.outer = size // INNER
        me = lax.axis_index(axis)
        self.me, self.mine, self.inner = me, me // INNER, me % INNER
        self.shard = out.shape[0]

    def owner(self, offset):
        return lax.rem(self.mine + offset, self.outer)

    def targets(self):
        far = [
            (self.axis, self.owner(offset) * INNER + self.inner, self.mine >= 0)
            for offset in range(1, self.outer)
        ]
        return far + [(self.axis, self.mine * INNER + 1 - self.inner, self.mine >= 0)]

    def near_copy(self, offset, chunk):
        owner = self.owner(offset)
        other = 1 - self.inner
        slot = owner * self.chunks + chunk
        return remote(
            self.data.at[piece(owner * INNER + other, chunk, self.chunks, self.shard)],
            self.near.at[piece(owner, chunk, self.chunks, self.shard)],
            self.near_send.at[slot],
            self.near_recv.at[slot],
            self.axis,
            self.mine * INNER + other,
        )

    def far_copy(self, offset, chunk):
        owner = self.owner(offset)
        return remote(
            self.near.at[piece(owner, chunk, self.chunks, self.shard)],
            self.far.at[piece(offset - 1, chunk, self.chunks, self.shard)],
            self.far_send.at[(offset - 1) * self.chunks + chunk],
            self.far_recv.at[(offset - 1) * self.chunks + chunk],
            self.axis,
            owner * INNER + self.inner,
        )

    def send_pair(self, offset, chunk):
        self.near_copy(offset, chunk).wait_recv()
        owner = self.owner(offset)
        size = self.shard // self.chunks
        near_at = (owner * self.chunks + chunk) * size
        data_at = ((owner * INNER + self.inner) * self.chunks + chunk) * size

        def add(index, carry):
            total = self.near[near_at + index].astype(jnp.float32)
            total += self.data[data_at + index].astype(jnp.float32)
            self.near[near_at + index] = total.astype(jnp.bfloat16)
            return carry

        lax.fori_loop(0, size, add, 0)
        self.far_copy(offset, chunk).start()

    def total(self, chunk):
        self.near_copy(0, chunk).wait_recv()
        for offset in range(1, self.outer):
            self.far_copy(offset, chunk).wait_recv()
        size = self.shard // self.chunks
        near_at = (self.mine * self.chunks + chunk) * size
        data_at = (self.me * self.chunks + chunk) * size

        def add(index, carry):
            total = self.near[near_at + index].astype(jnp.float32)
            total += self.data[data_at + index].astype(jnp.float32)
            for offset in range(1, self.outer):
                at = ((offset - 1) * self.chunks + chunk) * size
                total += self.far[at + index].astype(jnp.float32)
            self.out[chunk * size + index] = total.astype(self.out.dtype)
            return carry

        lax.fori_loop(0, size, add, 0)

    def finish(self):
        for chunk in range(self.chunks):
            for offset in range(self.outer):
                self.near_copy(offset, chunk).wait_send()
                if offset > 0:
                    self.far_copy(offset, chunk).wait_send()


def make_tiles(left_at, right_at, left_ref, right_ref, tiles_ref, first, count, scale):
    unroll = math.gcd(UNROLL, count)

    def step(index, carry):
        base = first + index * unroll
        for k in range(unroll):
            tile = lax.dot_general(
                left_ref[left_at[base + k]],
                right_ref[right_at[base + k]],
                (((0,), (0,)), ((), ())),
                preferred_element_type=jnp.float32,
            )
            tiles_ref[base + k] = (scale * tile).astype(jnp.bfloat16)
        return carry

    lax.fori_loop(0, count // unroll, step, 0)


def reduce_kernel(
    sizes,
    chunk_counts,
    scale,
    left_at,
    right_at,
    left_ref,
    right_ref,
    rows,
    grads_out,
    rows_out,
    tiles,
    *scratch,
):
    wide = PairReduce(
        "dp", sizes[0], chunk_counts[0], tiles, grads_out, scratch[0], scratch[1], scratch[4:8]
    )
    thin = PairReduce(
        "tensor", sizes[1], chunk_counts[1], rows, rows_out, scratch[2], scratch[3], scratch[8:]
    )
    greet(wide.targets() + thin.targets())
    for offset in list(range(1, thin.outer)) + [0]:
        for chunk in range(thin.chunks):
            thin.near_copy(offset, chunk).start()
    size = wide.shard // wide.chunks
    thin_pairs = [(o, k) for o in range(1, thin.outer) for k in range(thin.chunks)]
    wide_steps = [(o, k) for o in list(range(1, wide.outer)) + [0] for k in range(wide.chunks)]
    for at, (offset, chunk) in enumerate(wide_steps):
        owner = wide.owner(offset)
        for inner in (1 - wide.inner, wide.inner):
            first = ((owner * INNER + inner) * wide.chunks + chunk) * size
            make_tiles(left_at, right_at, left_ref, right_ref, tiles, first, size, scale)
            if inner is not wide.inner:
                wide.near_copy(offset, chunk).start()
        if offset > 0:
            wide.send_pair(offset, chunk)
        low = at * len(thin_pairs) // len(wide_steps)
        high = (at + 1) * len(thin_pairs) // len(wide_steps)
        for pair in thin_pairs[low:high]:
            thin.send_pair(*pair)
    for chunk in range(wide.chunks - 1):
        wide.total(chunk)
    for chunk in range(thin.chunks):
        thin.total(chunk)
    wide.total(wide.chunks - 1)
    wide.finish()
    thin.finish()


def pair_sems(size, chunks):
    dma = pltpu.SemaphoreType.DMA
    outer = size // INNER
    return [dma((outer * chunks,))] * 2 + [dma((max(outer - 1, 1) * chunks,))] * 2


def reduce_all(left_at, right_at, left_source, right_source, partial_rows, scale):
    sizes = (lax.axis_size("dp"), lax.axis_size("tensor"))
    side = left_source.shape[2]
    tile_shape = (left_at.shape[0], side, side)
    shards = (tile_shape[0] // sizes[0], partial_rows.shape[0] // sizes[1])
    chunk_counts = (math.gcd(4, shards[0]), math.gcd(2, shards[1]))
    vmem = pl.BlockSpec(memory_space=pltpu.VMEM)
    smem = pl.BlockSpec(memory_space=pltpu.SMEM)
    scratch = [pltpu.VMEM(tile_shape, jnp.bfloat16)]
    for shape, size, shard in zip((tile_shape, partial_rows.shape), sizes, shards):
        outer = size // INNER
        scratch.append(pltpu.VMEM((outer * shard,) + shape[1:], jnp.bfloat16))
        scratch.append(pltpu.VMEM((max(outer - 1, 1) * shard,) + shape[1:], jnp.bfloat16))
    return pl.pallas_call(
        functools.partial(reduce_kernel, sizes, chunk_counts, scale),
        out_shape=(
            jax.ShapeDtypeStruct((shards[0],) + tile_shape[1:], jnp.float32),
            jax.ShapeDtypeStruct((shards[1],) + partial_rows.shape[1:], jnp.bfloat16),
        ),
        in_specs=[smem, smem, vmem, vmem, vmem],
        out_specs=(vmem, vmem),
        scratch_shapes=scratch
        + pair_sems(sizes[0], chunk_counts[0])
        + pair_sems(sizes[1], chunk_counts[1]),
        compiler_params=pltpu.CompilerParams(
            collective_id=1, has_side_effects=True, vmem_limit_bytes=48 * 1024 * 1024
        ),
    )(left_at, right_at, left_source, right_source, partial_rows)


UNROLL = 8


def forward_kernel(
    left_at,
    right_at,
    sum_at,
    row_at,
    up_steps,
    packed_ref,
    left_ref,
    right_ref,
    out_ref,
    sums,
    row_sums,
    *,
    scale,
):
    slot_total = packed_ref.shape[0]
    columns = right_ref.shape[0] // 2

    def clear(index, carry):
        sums[index] = jnp.zeros(sums.shape[1:], jnp.float32)
        return carry

    lax.fori_loop(0, sums.shape[0], clear, 0)

    def add_slots(step, carry):
        base = step * UNROLL
        parts = [
            jnp.dot(
                left_ref[left_at[base + k]],
                packed_ref[base + k],
                preferred_element_type=jnp.float32,
            )
            for k in range(UNROLL)
        ]
        for k in range(UNROLL):
            sums[sum_at[base + k]] += parts[k]
        return carry

    lax.fori_loop(0, slot_total // UNROLL, add_slots, 0)

    def activate(column, carry):
        pre_act = scale * sums[column]
        back_act = scale * sums[columns + column]
        right_ref[column] = (back_act * silu_slope(pre_act)).astype(jnp.bfloat16)
        right_ref[columns + column] = jax.nn.silu(pre_act).astype(jnp.bfloat16)
        return carry

    lax.fori_loop(0, columns, activate, 0)

    add_input_grad(right_at, row_at, up_steps, packed_ref, right_ref, out_ref, row_sums, scale)


def add_input_grad(right_at, row_at, up_steps, packed_ref, right_ref, out_ref, sums, scale):
    rows = out_ref.shape[0]

    def clear(index, carry):
        sums[index] = jnp.zeros(sums.shape[1:], jnp.float32)
        return carry

    lax.fori_loop(0, rows, clear, 0)

    def add_slots(step, carry):
        base = step * UNROLL
        parts = [
            lax.dot_general(
                right_ref[right_at[base + k]],
                packed_ref[base + k],
                (((1,), (1,)), ((), ())),
                preferred_element_type=jnp.float32,
            )
            for k in range(UNROLL)
        ]
        for k in range(UNROLL):
            sums[row_at[base + k]] += parts[k]
        return carry

    lax.fori_loop(0, up_steps[0], add_slots, 0)

    def finish(index, carry):
        out_ref[index] = (scale * sums[index]).astype(jnp.bfloat16)
        return carry

    lax.fori_loop(0, rows, finish, 0)


def per_device(
    tokens,
    grad_out,
    packed_weight_blocks,
    packed_first_moments,
    packed_second_moments,
    block_mask,
    last_step,
    regrown,
    step_now,
):
    scale_factor = 3.0 / math.sqrt(D)
    tok_count = tokens.shape[0]
    owned_slots = packed_weight_blocks.shape[0]
    block_size = packed_weight_blocks.shape[1]
    row_blocks = block_mask.shape[1]
    column_blocks = block_mask.shape[2]
    local_rows = tokens.shape[1] // block_size
    groups = lax.axis_size("dp")
    slot_total = owned_slots * groups
    step_value = step_now[0]
    packed, left_source = gather_all(packed_weight_blocks, tokens, grad_out)
    block_index, slot_regrown, slot_last, live_count, up_count = slot_table(
        block_mask, regrown, last_step, slot_total
    )
    matrix_of = block_index // (row_blocks * column_blocks)
    row_of = block_index // column_blocks % row_blocks
    column_of = block_index % column_blocks
    slot_ids = jnp.arange(slot_total, dtype=jnp.int32)
    usable = (slot_ids < live_count) & (slot_regrown == 0)
    left_at = (row_of // local_rows * 2 + matrix_of) * local_rows + row_of % local_rows
    right_at = matrix_of * column_blocks + column_of
    sum_at = jnp.where(usable, right_at, 2 * column_blocks)
    row_at = jnp.where(usable & (matrix_of == 0), row_of, row_blocks)
    up_steps = ((up_count + UNROLL - 1) // UNROLL).reshape(1)
    smem = pl.BlockSpec(memory_space=pltpu.SMEM)
    vmem = pl.BlockSpec(memory_space=pltpu.VMEM)
    params = pltpu.CompilerParams(vmem_limit_bytes=48 * 1024 * 1024)
    block = (tok_count, block_size)
    right_source, partial_rows = pl.pallas_call(
        functools.partial(forward_kernel, scale=scale_factor),
        out_shape=(
            jax.ShapeDtypeStruct((2 * column_blocks,) + block, jnp.bfloat16),
            jax.ShapeDtypeStruct((row_blocks,) + block, jnp.bfloat16),
        ),
        in_specs=[smem] * 5 + [vmem] * 2,
        out_specs=(vmem, vmem),
        scratch_shapes=[
            pltpu.VMEM((2 * column_blocks + 1,) + block, jnp.float32),
            pltpu.VMEM((row_blocks + 1,) + block, jnp.float32),
        ],
        compiler_params=params,
    )(left_at, right_at, sum_at, row_at, up_steps, packed, left_source)
    block_grads, summed_rows = reduce_all(
        left_at, right_at, left_source, right_source, partial_rows, scale_factor
    )
    input_grad = (
        summed_rows.transpose(1, 0, 2).reshape(tok_count, tokens.shape[1]).astype(jnp.bfloat16)
    )
    owner_first = lax.axis_index("dp") * owned_slots
    mine_regrown = lax.dynamic_slice_in_dim(slot_regrown, owner_first, owned_slots)
    mine_last = lax.dynamic_slice_in_dim(slot_last, owner_first, owned_slots)
    live_slots = owner_first + jnp.arange(owned_slots, dtype=jnp.int32) < live_count
    new_weights, new_first, new_second = adam_step(
        packed_weight_blocks,
        packed_first_moments,
        packed_second_moments,
        block_grads,
        live_slots,
        mine_regrown,
        mine_last,
        step_value,
    )
    return (input_grad, new_weights, new_first, new_second)


def solution(mesh):
    in_specs = (
        P("dp", "tensor"),
        P("dp", "tensor"),
        P(("dp", "tensor"), None, None),
        P(("dp", "tensor"), None, None),
        P(("dp", "tensor"), None, None),
        P(None, None, "tensor"),
        P(None, None, "tensor"),
        P(None, None, "tensor"),
        P(),
    )
    out_specs = (
        P("dp", "tensor"),
        P(("dp", "tensor"), None, None),
        P(("dp", "tensor"), None, None),
        P(("dp", "tensor"), None, None),
    )
    return jax.shard_map(
        per_device, mesh=mesh, in_specs=in_specs, out_specs=out_specs, check_vma=False
    )
```

```python
import functools
import math

import jax
import jax.numpy as jnp
from jax import lax
from jax.experimental import pallas as pl
from jax.experimental.pallas import tpu as pltpu
from jax.sharding import PartitionSpec as P

D = 8192


beta_one = 0.9
beta_two = 0.95
learn_rate = 0.05
decay_rate = 0.1
epsilon = 0.05


def silu_slope(values):
    sigmoid = jax.nn.sigmoid(values)
    return sigmoid * (1.0 + values * (1.0 - sigmoid))


def slot_table(mask_grid, regrown_grid, last_grid, slot_total):
    codes = lax.optimization_barrier((mask_grid + 2 * regrown_grid + 4 * last_grid).reshape(-1))
    flags = codes & 1
    numbered = jnp.cumsum(flags, dtype=jnp.int32) - 1
    block_total = flags.shape[0]
    wanted = jnp.where(flags == 1, numbered, -1)
    entries = jnp.arange(block_total, dtype=jnp.int32) + block_total * (codes >> 1)
    matches = wanted[None, :] == jnp.arange(slot_total, dtype=jnp.int32)[:, None]
    found = lax.optimization_barrier(
        jnp.sum(jnp.where(matches, entries[None, :], 0), axis=1, dtype=jnp.int32)
    )
    block_index = found % block_total
    slot_regrown = found // block_total & 1
    slot_last = found // block_total // 2
    live_count = jnp.sum(flags, dtype=jnp.int32)
    up_count = jnp.sum(flags[: block_total // 2], dtype=jnp.int32)
    return (block_index, slot_regrown, slot_last, live_count, up_count)


def adam_step(
    weights, first_in, second_in, block_grads, live_slots, slot_regrown, slot_last, step_value
):
    regrown_now = (slot_regrown == 1)[:, None, None]
    skipped = (step_value - slot_last - 1).astype(jnp.float32)[:, None, None]
    base_weight = jnp.where(regrown_now, jnp.float32(0.0), weights)
    kept_first = jnp.where(
        regrown_now, jnp.float32(0.0), first_in * jnp.power(jnp.float32(beta_one), skipped)
    )
    kept_second = jnp.where(
        regrown_now, jnp.float32(0.0), second_in * jnp.power(jnp.float32(beta_two), skipped)
    )
    new_first = beta_one * kept_first + (1.0 - beta_one) * block_grads
    new_second = beta_two * kept_second + (1.0 - beta_two) * block_grads * block_grads
    bias_count = jnp.where(
        regrown_now, jnp.float32(1.0), step_value.astype(jnp.float32) + jnp.zeros_like(skipped)
    )
    first_hat = new_first / (1.0 - jnp.power(jnp.float32(beta_one), bias_count))
    second_hat = new_second / (1.0 - jnp.power(jnp.float32(beta_two), bias_count))
    new_weight = base_weight - learn_rate * (
        first_hat / (jnp.sqrt(second_hat) + epsilon) + decay_rate * base_weight
    )
    keep_slot = live_slots[:, None, None]
    return (
        jnp.where(keep_slot, new_weight, weights),
        jnp.where(keep_slot, new_first, first_in),
        jnp.where(keep_slot, new_second, second_in),
    )


INNER = 2


def piece(index, chunk, chunks, shard):
    size = shard // chunks
    return pl.ds((index * chunks + chunk) * size, size)


def remote(src, dst, send_sem, recv_sem, axis, target):
    return pltpu.make_async_remote_copy(
        src_ref=src,
        dst_ref=dst,
        send_sem=send_sem,
        recv_sem=recv_sem,
        device_id={axis: target},
        device_id_type=pl.DeviceIdType.MESH,
    )


def greet(targets, meanwhile=None):
    barrier = pltpu.get_barrier_semaphore()
    for axis, target, exists in targets:

        @pl.when(exists)
        def _(axis=axis, target=target):
            pl.semaphore_signal(
                barrier, inc=1, device_id={axis: target}, device_id_type=pl.DeviceIdType.MESH
            )

    if meanwhile is not None:
        meanwhile()
    pl.semaphore_wait(barrier, sum(jnp.where(exists, 1, 0) for _, _, exists in targets))


class LineGather:
    def __init__(self, axis, size, chunks, own, out, sems):
        self.axis, self.chunks, self.own, self.out = axis, chunks, own, out
        self.recv, self.up, self.down, self.across, self.local = sems
        self.outer = size // INNER
        me = lax.axis_index(axis)
        self.me, self.mine, self.inner = me, me // INNER, me % INNER
        self.shard = own.shape[0]

    def targets(self):
        mine = self.mine
        return [
            (self.axis, self.me + INNER, mine + 1 < self.outer),
            (self.axis, self.me - INNER, mine > 0),
            (self.axis, mine * INNER + 1 - self.inner, mine >= 0),
        ]

    def copy(self, source, chunk, way, inner=None):
        inner = self.inner if inner is None else inner
        index = source * INNER + inner
        at = self.out.at[piece(index, chunk, self.chunks, self.shard)]
        slot = source * self.chunks + chunk
        sem, target = {
            "up": (self.up, self.me + INNER),
            "down": (self.down, self.me - INNER),
            "across": (self.across, self.mine * INNER + 1 - self.inner),
        }[way]
        recv = self.recv.at[index * self.chunks + chunk]
        return at, sem.at[slot], recv, target

    def send(self, source, chunk, way, own=False):
        at, sem, recv, target = self.copy(source, chunk, way)
        src = self.own.at[piece(0, chunk, self.chunks, self.shard)] if own else at
        remote(src, at, sem, recv, self.axis, target).start()

    def wait_send(self, source, chunk, way):
        at, sem, recv, target = self.copy(source, chunk, way)
        remote(at, at, sem, recv, self.axis, target).wait_send()

    def wait_recv(self, source, chunk, inner):
        at, sem, recv, target = self.copy(source, chunk, "across", inner)
        remote(at, at, sem, recv, self.axis, target).wait_recv()

    def own_copy(self):
        at = self.out.at[pl.ds(self.me * self.shard, self.shard)]
        return pltpu.make_async_copy(self.own, at, self.local)

    def begin(self, chunk):
        mine = self.mine

        @pl.when(mine + 1 < self.outer)
        def _():
            self.send(mine, chunk, "up", own=True)

        @pl.when(mine > 0)
        def _():
            self.send(mine, chunk, "down", own=True)

        self.send(mine, chunk, "across", own=True)

    def step(self, distance, chunk):
        low, high = self.mine - distance, self.mine + distance

        @pl.when(low >= 0)
        def _():
            self.wait_recv(low, chunk, self.inner)

            @pl.when(self.mine + 1 < self.outer)
            def _():
                self.send(low, chunk, "up")

            self.send(low, chunk, "across")

        @pl.when(high < self.outer)
        def _():
            self.wait_recv(high, chunk, self.inner)

            @pl.when(self.mine > 0)
            def _():
                self.send(high, chunk, "down")

            self.send(high, chunk, "across")

    def finish(self):
        for source in range(self.outer):
            for chunk in range(self.chunks):
                self.wait_recv(source, chunk, 1 - self.inner)
                self.wait_send(source, chunk, "across")

                @pl.when((self.mine >= source) & (self.mine + 1 < self.outer))
                def _(source=source, chunk=chunk):
                    self.wait_send(source, chunk, "up")

                @pl.when((self.mine <= source) & (self.mine > 0))
                def _(source=source, chunk=chunk):
                    self.wait_send(source, chunk, "down")

        self.own_copy().wait()


def gather_kernel(
    sizes,
    chunk_counts,
    weights,
    tokens,
    grad_out,
    packed_out,
    left_out,
    own_packed,
    own_left,
    *sems,
):
    lines = [
        LineGather("dp", sizes[0], chunk_counts[0], own_packed, packed_out, sems[:5]),
        LineGather("tensor", sizes[1], chunk_counts[1], own_left, left_out, sems[5:]),
    ]

    def round_own():
        side = own_left.shape[2]
        local_rows = own_left.shape[0] // 2
        for row in range(local_rows):
            own_left[row] = tokens[:, row * side : (row + 1) * side]
            own_left[local_rows + row] = grad_out[:, row * side : (row + 1) * side]

        def round_block(index, carry):
            own_packed[index] = weights[index].astype(jnp.bfloat16)
            return carry

        lax.fori_loop(0, own_packed.shape[0], round_block, 0)

    greet(lines[0].targets() + lines[1].targets(), round_own)
    events = []
    for line, weight in zip(lines, (1.5, 1.0)):
        for chunk in range(line.chunks):
            events.append((chunk / line.chunks, line, 0, chunk))
            for distance in range(1, line.outer):
                passed = (distance - 1 + (chunk + 1) / line.chunks) / (line.outer - 1)
                when = 1 + weight * passed
                events.append((when, line, distance, chunk))
    events.sort(key=lambda event: event[0])
    for when, line, distance, chunk in events:
        if distance == 0:
            line.begin(chunk)
    for line in lines:
        line.own_copy().start()
    for when, line, distance, chunk in events:
        if distance > 0:
            line.step(distance, chunk)
    for line in lines:
        line.finish()


def line_sems(size, chunks):
    dma = pltpu.SemaphoreType.DMA
    outer = size // INNER
    return [dma((size * chunks,))] + [dma((outer * chunks,))] * 3 + [dma]


def gather_all(weights, tokens, grad_out):
    sizes = (lax.axis_size("dp"), lax.axis_size("tensor"))
    side = weights.shape[1]
    own_left = (2 * tokens.shape[1] // side, tokens.shape[0], side)
    chunk_counts = (math.gcd(8, weights.shape[0]), math.gcd(4, own_left[0]))
    vmem = pl.BlockSpec(memory_space=pltpu.VMEM)
    anywhere = pl.BlockSpec(memory_space=pl.ANY)
    return pl.pallas_call(
        functools.partial(gather_kernel, sizes, chunk_counts),
        out_shape=(
            jax.ShapeDtypeStruct((sizes[0] * weights.shape[0], side, side), jnp.bfloat16),
            jax.ShapeDtypeStruct((sizes[1] * own_left[0],) + own_left[1:], jnp.bfloat16),
        ),
        in_specs=[vmem, vmem, vmem],
        out_specs=(anywhere, anywhere),
        scratch_shapes=[
            pltpu.VMEM(weights.shape, jnp.bfloat16),
            pltpu.VMEM(own_left, jnp.bfloat16),
        ]
        + line_sems(sizes[0], chunk_counts[0])
        + line_sems(sizes[1], chunk_counts[1]),
        compiler_params=pltpu.CompilerParams(
            collective_id=0, has_side_effects=True, vmem_limit_bytes=48 * 1024 * 1024
        ),
    )(weights, tokens, grad_out)


class PairReduce:
    def __init__(self, axis, size, chunks, data, out, near, far, sems):
        self.axis, self.chunks, self.data, self.out = axis, chunks, data, out
        self.near, self.far = near, far
        self.near_send, self.near_recv, self.far_send, self.far_recv = sems
        self.outer = size // INNER
        me = lax.axis_index(axis)
        self.me, self.mine, self.inner = me, me // INNER, me % INNER
        self.shard = out.shape[0]

    def owner(self, offset):
        return lax.rem(self.mine + offset, self.outer)

    def targets(self):
        far = [
            (self.axis, self.owner(offset) * INNER + self.inner, self.mine >= 0)
            for offset in range(1, self.outer)
        ]
        return far + [(self.axis, self.mine * INNER + 1 - self.inner, self.mine >= 0)]

    def near_copy(self, offset, chunk):
        owner = self.owner(offset)
        other = 1 - self.inner
        slot = owner * self.chunks + chunk
        return remote(
            self.data.at[piece(owner * INNER + other, chunk, self.chunks, self.shard)],
            self.near.at[piece(owner, chunk, self.chunks, self.shard)],
            self.near_send.at[slot],
            self.near_recv.at[slot],
            self.axis,
            self.mine * INNER + other,
        )

    def far_copy(self, offset, chunk):
        owner = self.owner(offset)
        return remote(
            self.near.at[piece(owner, chunk, self.chunks, self.shard)],
            self.far.at[piece(offset - 1, chunk, self.chunks, self.shard)],
            self.far_send.at[(offset - 1) * self.chunks + chunk],
            self.far_recv.at[(offset - 1) * self.chunks + chunk],
            self.axis,
            owner * INNER + self.inner,
        )

    def send_pair(self, offset, chunk):
        self.near_copy(offset, chunk).wait_recv()
        owner = self.owner(offset)
        size = self.shard // self.chunks
        near_at = (owner * self.chunks + chunk) * size
        data_at = ((owner * INNER + self.inner) * self.chunks + chunk) * size

        def add(index, carry):
            total = self.near[near_at + index].astype(jnp.float32)
            total += self.data[data_at + index].astype(jnp.float32)
            self.near[near_at + index] = total.astype(jnp.bfloat16)
            return carry

        lax.fori_loop(0, size, add, 0)
        self.far_copy(offset, chunk).start()

    def total(self, chunk):
        self.near_copy(0, chunk).wait_recv()
        for offset in range(1, self.outer):
            self.far_copy(offset, chunk).wait_recv()
        size = self.shard // self.chunks
        near_at = (self.mine * self.chunks + chunk) * size
        data_at = (self.me * self.chunks + chunk) * size

        def add(index, carry):
            total = self.near[near_at + index].astype(jnp.float32)
            total += self.data[data_at + index].astype(jnp.float32)
            for offset in range(1, self.outer):
                at = ((offset - 1) * self.chunks + chunk) * size
                total += self.far[at + index].astype(jnp.float32)
            self.out[chunk * size + index] = total.astype(self.out.dtype)
            return carry

        lax.fori_loop(0, size, add, 0)

    def finish(self):
        for chunk in range(self.chunks):
            for offset in range(self.outer):
                self.near_copy(offset, chunk).wait_send()
                if offset > 0:
                    self.far_copy(offset, chunk).wait_send()


def make_tiles(left_at, right_at, left_ref, right_ref, tiles_ref, first, count, scale):
    unroll = math.gcd(UNROLL, count)

    def step(index, carry):
        base = first + index * unroll
        for k in range(unroll):
            tile = lax.dot_general(
                left_ref[left_at[base + k]],
                right_ref[right_at[base + k]],
                (((0,), (0,)), ((), ())),
                preferred_element_type=jnp.float32,
            )
            tiles_ref[base + k] = (scale * tile).astype(jnp.bfloat16)
        return carry

    lax.fori_loop(0, count // unroll, step, 0)


def reduce_kernel(
    sizes,
    chunk_counts,
    scale,
    left_at,
    right_at,
    left_ref,
    right_ref,
    rows,
    grads_out,
    rows_out,
    tiles,
    *scratch,
):
    wide = PairReduce(
        "dp", sizes[0], chunk_counts[0], tiles, grads_out, scratch[0], scratch[1], scratch[4:8]
    )
    thin = PairReduce(
        "tensor", sizes[1], chunk_counts[1], rows, rows_out, scratch[2], scratch[3], scratch[8:]
    )
    greet(wide.targets() + thin.targets())
    for offset in list(range(1, thin.outer)) + [0]:
        for chunk in range(thin.chunks):
            thin.near_copy(offset, chunk).start()
    size = wide.shard // wide.chunks
    thin_pairs = [(o, k) for o in range(1, thin.outer) for k in range(thin.chunks)]
    wide_steps = [(o, k) for o in list(range(1, wide.outer)) + [0] for k in range(wide.chunks)]
    for at, (offset, chunk) in enumerate(wide_steps):
        owner = wide.owner(offset)
        for inner in (1 - wide.inner, wide.inner):
            first = ((owner * INNER + inner) * wide.chunks + chunk) * size
            make_tiles(left_at, right_at, left_ref, right_ref, tiles, first, size, scale)
            if inner is not wide.inner:
                wide.near_copy(offset, chunk).start()
        if offset > 0:
            wide.send_pair(offset, chunk)
        low = at * len(thin_pairs) // len(wide_steps)
        high = (at + 1) * len(thin_pairs) // len(wide_steps)
        for pair in thin_pairs[low:high]:
            thin.send_pair(*pair)
    for chunk in range(wide.chunks - 1):
        wide.total(chunk)
    for chunk in range(thin.chunks):
        thin.total(chunk)
    wide.total(wide.chunks - 1)
    wide.finish()
    thin.finish()


def pair_sems(size, chunks):
    dma = pltpu.SemaphoreType.DMA
    outer = size // INNER
    return [dma((outer * chunks,))] * 2 + [dma((max(outer - 1, 1) * chunks,))] * 2


def reduce_all(left_at, right_at, left_source, right_source, partial_rows, scale):
    sizes = (lax.axis_size("dp"), lax.axis_size("tensor"))
    side = left_source.shape[2]
    tile_shape = (left_at.shape[0], side, side)
    shards = (tile_shape[0] // sizes[0], partial_rows.shape[0] // sizes[1])
    chunk_counts = (math.gcd(8, shards[0]), math.gcd(2, shards[1]))
    vmem = pl.BlockSpec(memory_space=pltpu.VMEM)
    smem = pl.BlockSpec(memory_space=pltpu.SMEM)
    scratch = [pltpu.VMEM(tile_shape, jnp.bfloat16)]
    for shape, size, shard in zip((tile_shape, partial_rows.shape), sizes, shards):
        outer = size // INNER
        scratch.append(pltpu.VMEM((outer * shard,) + shape[1:], jnp.bfloat16))
        scratch.append(pltpu.VMEM((max(outer - 1, 1) * shard,) + shape[1:], jnp.bfloat16))
    return pl.pallas_call(
        functools.partial(reduce_kernel, sizes, chunk_counts, scale),
        out_shape=(
            jax.ShapeDtypeStruct((shards[0],) + tile_shape[1:], jnp.float32),
            jax.ShapeDtypeStruct((shards[1],) + partial_rows.shape[1:], jnp.bfloat16),
        ),
        in_specs=[smem, smem, vmem, vmem, vmem],
        out_specs=(vmem, vmem),
        scratch_shapes=scratch
        + pair_sems(sizes[0], chunk_counts[0])
        + pair_sems(sizes[1], chunk_counts[1]),
        compiler_params=pltpu.CompilerParams(
            collective_id=1, has_side_effects=True, vmem_limit_bytes=48 * 1024 * 1024
        ),
    )(left_at, right_at, left_source, right_source, partial_rows)


UNROLL = 8


def forward_kernel(
    left_at,
    right_at,
    sum_at,
    row_at,
    up_steps,
    packed_ref,
    left_ref,
    right_ref,
    out_ref,
    sums,
    row_sums,
    *,
    scale,
):
    slot_total = packed_ref.shape[0]
    columns = right_ref.shape[0] // 2

    def clear(index, carry):
        sums[index] = jnp.zeros(sums.shape[1:], jnp.float32)
        return carry

    lax.fori_loop(0, sums.shape[0], clear, 0)

    def add_slots(step, carry):
        base = step * UNROLL
        parts = [
            jnp.dot(
                left_ref[left_at[base + k]],
                packed_ref[base + k],
                preferred_element_type=jnp.float32,
            )
            for k in range(UNROLL)
        ]
        for k in range(UNROLL):
            sums[sum_at[base + k]] += parts[k]
        return carry

    lax.fori_loop(0, slot_total // UNROLL, add_slots, 0)

    def activate(column, carry):
        pre_act = scale * sums[column]
        back_act = scale * sums[columns + column]
        right_ref[column] = (back_act * silu_slope(pre_act)).astype(jnp.bfloat16)
        right_ref[columns + column] = jax.nn.silu(pre_act).astype(jnp.bfloat16)
        return carry

    lax.fori_loop(0, columns, activate, 0)

    add_input_grad(right_at, row_at, up_steps, packed_ref, right_ref, out_ref, row_sums, scale)


def add_input_grad(right_at, row_at, up_steps, packed_ref, right_ref, out_ref, sums, scale):
    rows = out_ref.shape[0]

    def clear(index, carry):
        sums[index] = jnp.zeros(sums.shape[1:], jnp.float32)
        return carry

    lax.fori_loop(0, rows, clear, 0)

    def add_slots(step, carry):
        base = step * UNROLL
        parts = [
            lax.dot_general(
                right_ref[right_at[base + k]],
                packed_ref[base + k],
                (((1,), (1,)), ((), ())),
                preferred_element_type=jnp.float32,
            )
            for k in range(UNROLL)
        ]
        for k in range(UNROLL):
            sums[row_at[base + k]] += parts[k]
        return carry

    lax.fori_loop(0, up_steps[0], add_slots, 0)

    def finish(index, carry):
        out_ref[index] = (scale * sums[index]).astype(jnp.bfloat16)
        return carry

    lax.fori_loop(0, rows, finish, 0)


def per_device(
    tokens,
    grad_out,
    packed_weight_blocks,
    packed_first_moments,
    packed_second_moments,
    block_mask,
    last_step,
    regrown,
    step_now,
):
    scale_factor = 3.0 / math.sqrt(D)
    tok_count = tokens.shape[0]
    owned_slots = packed_weight_blocks.shape[0]
    block_size = packed_weight_blocks.shape[1]
    row_blocks = block_mask.shape[1]
    column_blocks = block_mask.shape[2]
    local_rows = tokens.shape[1] // block_size
    groups = lax.axis_size("dp")
    slot_total = owned_slots * groups
    step_value = step_now[0]
    packed, left_source = gather_all(packed_weight_blocks, tokens, grad_out)
    block_index, slot_regrown, slot_last, live_count, up_count = slot_table(
        block_mask, regrown, last_step, slot_total
    )
    matrix_of = block_index // (row_blocks * column_blocks)
    row_of = block_index // column_blocks % row_blocks
    column_of = block_index % column_blocks
    slot_ids = jnp.arange(slot_total, dtype=jnp.int32)
    usable = (slot_ids < live_count) & (slot_regrown == 0)
    left_at = (row_of // local_rows * 2 + matrix_of) * local_rows + row_of % local_rows
    right_at = matrix_of * column_blocks + column_of
    sum_at = jnp.where(usable, right_at, 2 * column_blocks)
    row_at = jnp.where(usable & (matrix_of == 0), row_of, row_blocks)
    up_steps = ((up_count + UNROLL - 1) // UNROLL).reshape(1)
    smem = pl.BlockSpec(memory_space=pltpu.SMEM)
    vmem = pl.BlockSpec(memory_space=pltpu.VMEM)
    params = pltpu.CompilerParams(vmem_limit_bytes=48 * 1024 * 1024)
    block = (tok_count, block_size)
    right_source, partial_rows = pl.pallas_call(
        functools.partial(forward_kernel, scale=scale_factor),
        out_shape=(
            jax.ShapeDtypeStruct((2 * column_blocks,) + block, jnp.bfloat16),
            jax.ShapeDtypeStruct((row_blocks,) + block, jnp.bfloat16),
        ),
        in_specs=[smem] * 5 + [vmem] * 2,
        out_specs=(vmem, vmem),
        scratch_shapes=[
            pltpu.VMEM((2 * column_blocks + 1,) + block, jnp.float32),
            pltpu.VMEM((row_blocks + 1,) + block, jnp.float32),
        ],
        compiler_params=params,
    )(left_at, right_at, sum_at, row_at, up_steps, packed, left_source)
    block_grads, summed_rows = reduce_all(
        left_at, right_at, left_source, right_source, partial_rows, scale_factor
    )
    input_grad = (
        summed_rows.transpose(1, 0, 2).reshape(tok_count, tokens.shape[1]).astype(jnp.bfloat16)
    )
    owner_first = lax.axis_index("dp") * owned_slots
    mine_regrown = lax.dynamic_slice_in_dim(slot_regrown, owner_first, owned_slots)
    mine_last = lax.dynamic_slice_in_dim(slot_last, owner_first, owned_slots)
    live_slots = owner_first + jnp.arange(owned_slots, dtype=jnp.int32) < live_count
    new_weights, new_first, new_second = adam_step(
        packed_weight_blocks,
        packed_first_moments,
        packed_second_moments,
        block_grads,
        live_slots,
        mine_regrown,
        mine_last,
        step_value,
    )
    return (input_grad, new_weights, new_first, new_second)


def solution(mesh):
    in_specs = (
        P("dp", "tensor"),
        P("dp", "tensor"),
        P(("dp", "tensor"), None, None),
        P(("dp", "tensor"), None, None),
        P(("dp", "tensor"), None, None),
        P(None, None, "tensor"),
        P(None, None, "tensor"),
        P(None, None, "tensor"),
        P(),
    )
    out_specs = (
        P("dp", "tensor"),
        P(("dp", "tensor"), None, None),
        P(("dp", "tensor"), None, None),
        P(("dp", "tensor"), None, None),
    )
    return jax.shard_map(
        per_device, mesh=mesh, in_specs=in_specs, out_specs=out_specs, check_vma=False
    )
```
